32 devices in a mesh: dp: 16 (over z, y, core), query: 2 (over x).
Axes of the slice: x: 2, y: 2, z: 4, core: 2. Of those that a mesh axis runs over, the one named last changes fastest.
Arguments:
- tokens: bfloat16 [2, 32, 128, 1280], P(None, ('dp', 'query')), may hold values from -6 to 6
- out_cotangent: bfloat16 [2, 32, 128, 1280], P(None, ('dp', 'query')), may hold values from -6 to 6
- qkv_weight: bfloat16 [1280, 3840], P('dp'), may hold values from -0.15625 to 0.15625
- out_weight: bfloat16 [1280, 1280], P('dp'), may hold values from -0.625 to 0.625
- up_weight: bfloat16 [1280, 5120], P('dp'), may hold values from -0.15625 to 0.15625
- down_weight: bfloat16 [5120, 1280], P('dp'), may hold values from -0.078125 to 0.078125
- attn_gain: bfloat16 [1280], P('dp'), may hold values from 0.5 to 1.5
- ffn_gain: bfloat16 [1280], P('dp'), may hold values from 0.5 to 1.5
- up_bias: bfloat16 [5120], P('dp'), may hold values from -3 to 3
- cell_weight: bfloat16 [1280, 5120], P('dp'), may hold values from -0.15625 to 0.15625
- gene_weight: bfloat16 [1280, 5120], P('dp'), may hold values from -0.15625 to 0.15625
- decoder_bias: bfloat16 [5120], P('dp'), may hold values from -3 to 3
- readout: bfloat16 [5120], P('dp'), may hold values from -0.15625 to 0.15625
- gene_embed: bfloat16 [2, 32, 384, 1280], P(None, ('dp', 'query')), may hold values from -6 to 6
- query_cell: int32 [2, 32, 384], P(None, ('dp', 'query')), may hold values from 0 to 1
- query_label: int32 [2, 32, 384], P(None, ('dp', 'query')), may hold values 0 or 1
- query_live: int32 [16, 2, 2], P('dp', None, 'query'), may hold values from 1 to 384, 480 in all within a row
Outputs:
- block_out: bfloat16 [2, 32, 128, 1280], P(None, ('dp', 'query'))
- grad_tokens: float32 [2, 32, 128, 1280], P(None, ('dp', 'query'))
- grad_qkv: float32 [1280, 3840], P('dp')
- grad_out: float32 [1280, 1280], P('dp')
- grad_up: float32 [1280, 5120], P('dp')
- grad_down: float32 [5120, 1280], P('dp')
- grad_attn_gain: float32 [1280], P('dp')
- grad_ffn_gain: float32 [1280], P('dp')
- grad_up_bias: float32 [5120], P('dp')
- grad_cell: float32 [1280, 5120], P('dp')
- grad_gene: float32 [1280, 5120], P('dp')
- grad_decoder_bias: float32 [5120], P('dp')
- grad_readout: float32 [5120], P('dp')
The draws below stay inside these ranges and needn't reach their ends.
Inputs may be any that keep to these rules, and one draw needn't show every extreme that they name: `query_live`: the 2 devices of one dp index together hold 480 live rows in each micro-batch; a device's live rows are its first slots. `query_cell`: index of a cell within the query group of the row's device.
All inputs are finite; a program needn't handle non-finite values. No bound on the sum of `query_label` on one device may be relied on, other than what follows from the above.
Results may differ from the reference program's by a relative error of at most 0.02.
Values may be sent and summed in bfloat16 or wider, within the bound.
No kernel may reach another device: no remote copies, remote signals or barrier semaphores. Data moves between devices by JAX's collectives and lax.ppermute only.
A program may use at most 320 MiB of HBM per device.

```python
import math
import jax
import jax.numpy as jnp
import numpy as np
from jax import lax

D = 1280
HEADS = 20
HEAD = 64
FF = 5120
DH = 5120
MB = 2
SEQ = 128
QR = 384
CELLS = 32
LIVE = 480
N_DP = 16
N_QUERY = 2


def plant(drawn, own_key, least, top_value):
    place = [jax.random.randint(jax.random.fold_in(own_key, axis), (), 0, length) for axis, length in enumerate(drawn.shape)]
    widest = drawn.shape.index(max(drawn.shape))
    neighbour = place[:widest] + [(place[widest] + 1) % drawn.shape[widest]] + place[widest + 1:]
    return drawn.at[tuple(place)].set(least).at[tuple(neighbour)].set(top_value)


def spiked(drawn, stream_key, source, target, parts, factor):
    def block_of(dim):
        return (jnp.arange(drawn.shape[dim]) // (drawn.shape[dim] // parts)).reshape((-1,) + (1,) * (drawn.ndim - 1 - dim))

    first = jax.random.permutation(stream_key, parts)[block_of(target)]
    second = (block_of(target) + parts // 2) % parts
    return jnp.where((block_of(source) == first) | (block_of(source) == second), factor * drawn, drawn)


def steps_of(own_key, dims, cuts, least, top_value):
    factor_of, own = 1.0, jax.random.fold_in(own_key, 6)
    for dim, shards_of in cuts:
        draws = jnp.exp(jax.random.uniform(jax.random.fold_in(own, dim), (shards_of,), jnp.float32, least / len(cuts), top_value / len(cuts)))
        factor_of = factor_of * jnp.repeat(draws, dims[dim] // shards_of).reshape([-1 if axis == dim else 1 for axis in range(len(dims))])
    return factor_of


def profile(number_of, total, reach, slope):
    weights = [(1 << 20) // math.isqrt(rank ** slope) + 1 for rank in range(2, number_of + 1)]
    rest, holding = total - reach - (number_of - 1), [1] * (number_of - 1)
    while rest > 0:
        candidates = [i for i in range(number_of - 1) if holding[i] < reach]
        mass, remaining = sum([weights[i] for i in candidates]), rest
        for i in candidates:
            addition = min(reach - holding[i], max(1, remaining * weights[i] // mass), rest)
            holding[i] = holding[i] + addition
            rest = rest - addition
    return np.array([reach] + holding)


def uneven(key, count, total, reach, slope):
    if count == 2:
        one = jax.random.randint(key, (), max(1, total - reach), min(reach, total - 1) + 1)
        return jnp.stack([one, total - one])
    lengths = jnp.asarray(profile(count, total, reach, slope), jnp.int32)
    couples = (count - 1) // 2
    source_of, sink = lengths[1:1 + 2 * couples:2], lengths[2:2 + 2 * couples:2]
    margin = jnp.minimum(source_of - 1, reach - sink)
    passed = jax.random.randint(jax.random.fold_in(key, 1), (couples,), 0, 1 << 20) % (margin + 1)
    lengths = lengths.at[1:1 + 2 * couples:2].set(source_of - passed).at[2:2 + 2 * couples:2].set(sink + passed)
    return lengths[jax.random.permutation(jax.random.fold_in(key, 2), count)]


def noise(stream_key, extent, spread, most, shards=(), kind=jnp.bfloat16):
    result = spread * jax.random.normal(stream_key, extent, jnp.float32)
    if shards:
        result = result * steps_of(stream_key, extent, shards, -0.22, 0.18)
    return jnp.clip(result, -most, most).astype(kind)


def noise_with(rng, shape, spread, limit, split, heavy, held_as=jnp.bfloat16):
    values = spread * jax.random.normal(rng, shape, jnp.float32)
    if split:
        values = values * steps_of(rng, shape, split, -0.22, 0.18)
    return jnp.clip(spiked(values, jax.random.fold_in(rng, 3), *heavy), -limit, limit).astype(held_as)


def setup_inputs(seed: int = 0) -> dict:
    arg_keys = jax.random.split(jax.random.key(seed), 18)
    tokens = noise_with(arg_keys[0], (MB, CELLS, SEQ, D), 1.0, 6.0, ((1, 32),), (1, 3, 32, 2.75))
    out_cotangent = noise(arg_keys[1], (MB, CELLS, SEQ, D), 1.0, 6.0, ((1, 32),))
    qkv_weight = noise(arg_keys[2], (D, 3 * D), D ** -0.5, 0.15625, ((0, 16),))
    out_weight = noise(arg_keys[3], (D, D), (D // 16) ** -0.5, 0.625, ((0, 16),))
    up_weight = noise(arg_keys[4], (D, FF), D ** -0.5, 0.15625, ((0, 16),))
    down_weight = noise(arg_keys[5], (FF, D), FF ** -0.5, 0.078125, ((0, 16),))
    attn_gain = jnp.clip(1.0 + 0.1 * jax.random.normal(arg_keys[6], (D,), jnp.float32), 0.5, 1.5).astype(jnp.bfloat16)
    ffn_gain = jnp.clip(1.0 + 0.1 * jax.random.normal(arg_keys[7], (D,), jnp.float32), 0.5, 1.5).astype(jnp.bfloat16)
    up_bias = noise(arg_keys[8], (FF,), 0.5, 3.0, ((0, 16),))
    cell_weight = noise(arg_keys[9], (D, DH), D ** -0.5, 0.15625, ((0, 16),))
    gene_weight = noise(arg_keys[10], (D, DH), D ** -0.5, 0.15625, ((0, 16),))
    decoder_bias = noise(arg_keys[11], (DH,), 0.5, 3.0, ((0, 16),))
    readout = noise(arg_keys[12], (DH,), (DH // 4) ** -0.5, 0.15625, ((0, 16),))
    gene_embed = noise(arg_keys[13], (MB, CELLS, QR, D), 1.0, 6.0, ((1, 32),))
    query_cell = plant(jax.random.randint(arg_keys[14], (MB, CELLS, QR), 0, N_QUERY), jax.random.fold_in(arg_keys[14], 1), 0, N_QUERY - 1).astype(jnp.int32)
    query_label = plant((jax.random.randint(arg_keys[15], (MB, CELLS, QR), 0, 2) < 1).astype(jnp.int32), jax.random.fold_in(arg_keys[15], 1), 0, 1)
    query_live = jax.vmap(lambda own: uneven(own, N_QUERY, LIVE, QR, 2))(jax.random.split(arg_keys[16], N_DP * MB)).reshape((N_DP, MB, N_QUERY)).astype(jnp.int32)
    return {"tokens": tokens, "out_cotangent": out_cotangent, "qkv_weight": qkv_weight, "out_weight": out_weight, "up_weight": up_weight, "down_weight": down_weight, "attn_gain": attn_gain, "ffn_gain": ffn_gain, "up_bias": up_bias, "cell_weight": cell_weight, "gene_weight": gene_weight, "decoder_bias": decoder_bias, "readout": readout, "gene_embed": gene_embed, "query_cell": query_cell, "query_label": query_label, "query_live": query_live}


@jax.custom_vjp
def low(v):
    return lax.optimization_barrier(v.astype(jnp.bfloat16)).astype(jnp.float32)

@jax.custom_vjp
def low_back(v):
    return v

def low_keep(v):
    return (low(v), None)

def low_pass(kept, grad):
    return (grad,)

def back_keep(v):
    return (v, None)

def back_low(kept, grad):
    return (low(grad),)
low.defvjp(low_keep, low_pass)
low_back.defvjp(back_keep, back_low)
highest = lax.Precision.HIGHEST
epsilon = 1e-05

def matmul(left, right):
    return jnp.matmul(left, right, precision=highest)

def layer_norm(values, gain):
    average = lax.optimization_barrier(jnp.mean(values, axis=-1, keepdims=True))
    centred = values - average
    variance = lax.optimization_barrier(jnp.mean(centred * centred, axis=-1, keepdims=True))
    return centred * lax.rsqrt(variance + epsilon) * gain

def attend_cell(block):
    queries, key_heads, value_heads = block
    scores = jnp.einsum('qhd,khd->hqk', queries, key_heads, precision=highest)
    scores = low_back(scores) * 0.125
    attn_probs = low(jax.nn.softmax(scores, axis=-1))
    return jnp.einsum('hqk,khd->qhd', attn_probs, value_heads, precision=highest)

def encoder(inputs, qkv_weight, out_weight, up_weight, down_weight, attn_gain, ffn_gain, up_bias):
    count = inputs.shape[0]
    normed = low(layer_norm(inputs, attn_gain))
    projected = low(low_back(matmul(normed, qkv_weight)))
    projected = projected.reshape(count, SEQ, 3, HEADS, HEAD)
    mixed_heads = lax.map(jax.checkpoint(attend_cell), (projected[:, :, 0], projected[:, :, 1], projected[:, :, 2]))
    mixed_heads = low(low_back(mixed_heads.reshape(count, SEQ, D)))
    hidden = inputs + low_back(matmul(mixed_heads, out_weight))
    second = low(layer_norm(hidden, ffn_gain))
    up_proj = low_back(matmul(second, up_weight) + up_bias)
    active = low(jax.nn.gelu(up_proj, approximate=True))
    return hidden + low_back(matmul(active, down_weight))

def reference(tokens, out_cotangent, qkv_weight, out_weight, up_weight, down_weight, attn_gain, ffn_gain, up_bias, cell_weight, gene_weight, decoder_bias, readout, gene_embed, query_cell, query_label, query_live):
    params = (qkv_weight, out_weight, up_weight, down_weight, attn_gain, ffn_gain, up_bias, cell_weight, gene_weight, decoder_bias, readout)
    params = tuple((weight.astype(jnp.float32) for weight in params))
    base_cell = jnp.arange(CELLS, dtype=jnp.int32) // N_QUERY * N_QUERY
    chosen = query_cell.astype(jnp.int32) + base_cell[None, :, None]
    micro_base = (jnp.arange(MB, dtype=jnp.int32) * CELLS)[:, None, None]
    chosen = (chosen + micro_base).reshape(MB * CELLS * QR)
    gene_rows = gene_embed.reshape(MB * CELLS * QR, D).astype(jnp.float32)
    live_rows = jnp.transpose(query_live, (1, 0, 2)).reshape(MB, CELLS)
    positions = jnp.arange(QR, dtype=jnp.int32)
    live_mask = (positions[None, None, :] < live_rows[:, :, None]).astype(jnp.float32).reshape(MB * CELLS * QR)
    labels = query_label.astype(jnp.float32).reshape(MB * CELLS * QR)

    def forward(inputs, *weights):
        qkv_w, out_w, up_w, down_w, gain_one, gain_two, bias_one, cell_w, gene_w, bias_two, read_w = weights
        flat = inputs.reshape(MB * CELLS, SEQ, D)
        output = encoder(flat, qkv_w, out_w, up_w, down_w, gain_one, gain_two, bias_one).reshape(MB, CELLS, SEQ, D)
        summary = low(output[:, :, 0, :]).reshape(MB * CELLS, D)
        cell_part = matmul(summary, cell_w)
        picked = jnp.take(cell_part, chosen, axis=0)
        pre_act = low_back(picked + matmul(gene_rows, gene_w) + bias_two)
        activity = jax.nn.silu(pre_act)
        logits = lax.optimization_barrier(jnp.sum(activity * read_w, axis=-1))
        loss_terms = jnp.logaddexp(0.0, logits) - labels * logits
        return (output, jnp.sum(loss_terms * live_mask))
    (output, loss_total), pullback = jax.vjp(forward, tokens.astype(jnp.float32), *params)
    grads = pullback((out_cotangent.astype(jnp.float32), jnp.ones_like(loss_total)))
    return (output.astype(jnp.bfloat16), grads[0], grads[1], grads[2], grads[3], grads[4], grads[5], grads[6], grads[7], grads[8], grads[9], grads[10], grads[11])
```

```python
import functools

import jax
import jax.numpy as jnp
from jax import lax
from jax.experimental import pallas as pl
from jax.experimental.pallas import tpu as pltpu
from jax.sharding import PartitionSpec as P

HEAD = 64
EPSILON = 1e-05
F32 = jnp.float32
BF16 = jnp.bfloat16


def product(left, right):
    return jnp.dot(left, right, preferred_element_type=F32)


def row_product(left, right):
    return lax.dot_general(left, right, (((0,), (0,)), ((), ())), preferred_element_type=F32)


def times_transpose(left, right):
    return lax.dot_general(left, right, (((1,), (1,)), ((), ())), preferred_element_type=F32)


def layer_stats(values):
    average = jnp.mean(values, axis=-1, keepdims=True)
    centred = values - average
    variance = jnp.mean(centred * centred, axis=-1, keepdims=True)
    inverse = lax.rsqrt(variance + EPSILON)
    return (centred * inverse, inverse)


def norm_back(grad_scaled, gain, normal, inverse):
    grad_normal = grad_scaled * gain
    along_normal = jnp.mean(grad_normal * normal, axis=-1, keepdims=True)
    average = jnp.mean(grad_normal, axis=-1, keepdims=True)
    grad_values = inverse * (grad_normal - average - normal * along_normal)
    return (grad_values, jnp.sum(grad_scaled * normal, axis=0))


def softmax_of(queries, keys):
    scores = times_transpose(queries, keys) * 0.125
    row_max = jnp.max(scores, axis=-1, keepdims=True)
    shifted = jnp.exp(scores - row_max)
    return shifted / jnp.sum(shifted, axis=-1, keepdims=True)


def attend_kernel(projected_ref, mixed_ref):
    width = mixed_ref.shape[1]
    for start in range(0, width, HEAD):
        queries = projected_ref[:, start : start + HEAD]
        keys = projected_ref[:, width + start : width + start + HEAD]
        values = projected_ref[:, 2 * width + start : 2 * width + start + HEAD]
        probs = softmax_of(queries, keys).astype(BF16)
        mixed_ref[:, start : start + HEAD] = product(probs, values).astype(BF16)


def attend_back_kernel(projected_ref, grad_mixed_ref, first_ref, grad_ref):
    width = grad_mixed_ref.shape[1]
    is_first = lax.broadcasted_iota(jnp.int32, (grad_mixed_ref.shape[0], HEAD), 0) == 0
    for start in range(0, width, HEAD):
        queries = projected_ref[:, start : start + HEAD]
        keys = projected_ref[:, width + start : width + start + HEAD]
        values = projected_ref[:, 2 * width + start : 2 * width + start + HEAD]
        grad_mixed = jnp.where(
            is_first, first_ref[0, :, start : start + HEAD], grad_mixed_ref[:, start : start + HEAD]
        )
        probs = softmax_of(queries, keys)
        grad_values = row_product(probs.astype(BF16), grad_mixed)
        grad_probs = times_transpose(grad_mixed, values)
        along = jnp.sum(grad_probs * probs, axis=-1, keepdims=True)
        grad_scores = (probs * (grad_probs - along) * 0.125).astype(BF16)
        grad_queries = product(grad_scores, keys)
        grad_keys = row_product(grad_scores, queries)
        grad_ref[:, start : start + HEAD] = grad_queries.astype(BF16)
        grad_ref[:, width + start : width + start + HEAD] = grad_keys.astype(BF16)
        grad_ref[:, 2 * width + start : 2 * width + start + HEAD] = grad_values.astype(BF16)


def attend(projected, length, first, count):
    rows, wide = count * length, projected.shape[1]
    return pl.pallas_call(
        attend_kernel,
        grid=(count,),
        in_specs=[pl.BlockSpec((length, wide), lambda i: (first + i, 0))],
        out_specs=pl.BlockSpec((length, wide // 3), lambda i: (i, 0)),
        out_shape=jax.ShapeDtypeStruct((rows, wide // 3), BF16),
        cost_estimate=pl.CostEstimate(
            flops=4 * rows * length * wide // 3,
            bytes_accessed=rows * wide * 3,
            transcendentals=rows * length * wide // 3 // HEAD,
        ),
    )(projected)


def attend_back(projected, grad_mixed, first, length):
    rows, wide = projected.shape
    return pl.pallas_call(
        attend_back_kernel,
        grid=(rows // length,),
        in_specs=[
            pl.BlockSpec((length, wide), lambda i: (i, 0)),
            pl.BlockSpec((length, wide // 3), lambda i: (i, 0)),
            pl.BlockSpec((1, 1, wide // 3), lambda i: (i, 0, 0)),
        ],
        out_specs=pl.BlockSpec((length, wide), lambda i: (i, 0)),
        out_shape=jax.ShapeDtypeStruct((rows, wide), BF16),
        cost_estimate=pl.CostEstimate(
            flops=10 * rows * length * wide // 3,
            bytes_accessed=rows * wide * 5,
            transcendentals=rows * length * wide // 3 // HEAD,
        ),
    )(projected, grad_mixed, first)


def ring_chip(position, chips):
    position = lax.rem(position + 2 * chips, chips)
    return jnp.where(position < chips // 2, 2 * position, 2 * (chips - 1 - position) + 1)


def place_kernel(segments, position_ref, *refs):
    count = (len(refs) - len(segments)) // 2
    outs = refs[2 * count :]
    for step in range(count):
        for side in range(2):
            piece = refs[2 * step + side]
            source = ring_chip(position_ref[0] + (step if side else -step), count)
            begin = 0
            for out, rows in zip(outs, segments):
                start = pl.multiple_of((2 * source + side) * rows, rows)
                out[pl.ds(start, rows), :] = piece[pl.ds(begin, rows), :]
                begin += rows


def place(pieces, position, segments):
    tall, wide = pieces[0].shape
    whole = pl.BlockSpec(memory_space=pltpu.VMEM)
    return pl.pallas_call(
        functools.partial(place_kernel, segments),
        in_specs=[pl.BlockSpec(memory_space=pltpu.SMEM)] + [whole] * len(pieces),
        out_specs=[whole] * len(segments),
        out_shape=[jax.ShapeDtypeStruct((len(pieces) * rows, wide), BF16) for rows in segments],
        cost_estimate=pl.CostEstimate(
            flops=0, bytes_accessed=4 * len(pieces) * tall * wide, transcendentals=0
        ),
        compiler_params=pltpu.CompilerParams(vmem_limit_bytes=32 << 20),
    )(position.reshape(1), *pieces)


def column_places(kind, part, n_dp):
    if kind == "attention":
        model = 4 * part
        return [
            [(0, i * model + k * part, i * part, part) for i in range(3)] + [(1, k * part, 3 * part, part)]
            for k in range(4)
        ]
    width = part // n_dp
    return [[(0, (4 * i + k) * width, i * width, width) for i in range(n_dp)] for k in range(4)]


def join_kernel(places, index_ref, *refs):
    blocks = [ref[...].astype(F32) for ref in refs[:4]]
    core, half = index_ref[0], index_ref[1]

    def swap(index, i, j):
        first = jnp.where(index == 0, blocks[i], blocks[j])
        blocks[j] = jnp.where(index == 0, blocks[j], blocks[i])
        blocks[i] = first

    swap(core, 0, 1)
    swap(core, 2, 3)
    swap(half, 0, 2)
    swap(half, 1, 3)
    for block, moves in zip(blocks, places):
        for output, start, source, width in moves:
            refs[4 + output][:, start : start + width] = block[:, source : source + width]


def join(blocks, index, places, widths):
    rows = blocks[0].shape[0]
    whole = pl.BlockSpec(memory_space=pltpu.VMEM)
    return pl.pallas_call(
        functools.partial(join_kernel, places),
        in_specs=[pl.BlockSpec(memory_space=pltpu.SMEM)] + [whole] * 4,
        out_specs=[whole] * len(widths),
        out_shape=[jax.ShapeDtypeStruct((rows, width), F32) for width in widths],
        cost_estimate=pl.CostEstimate(
            flops=0, bytes_accessed=6 * rows * sum(widths), transcendentals=0
        ),
        compiler_params=pltpu.CompilerParams(vmem_limit_bytes=32 << 20),
    )(index, *blocks)


def split_first_kernel(n_dp, index_ref, qkv_ref, out_ref, up_ref, *refs):
    vectors, targets = refs[:-2], refs[-2:]
    rows, part = out_ref.shape[0], out_ref.shape[1] // 4
    width = up_ref.shape[1] // 4 // n_dp
    for k in range(4):
        for flip, target in enumerate(targets):

            @pl.when(index_ref[0] == k ^ flip)
            def _():
                for i in range(3):
                    target[0:rows, i * part : (i + 1) * part] = qkv_ref[
                        :, (4 * i + k) * part : (4 * i + k + 1) * part
                    ]
                target[0:rows, 3 * part :] = out_ref[:, k * part : (k + 1) * part]
                for i in range(n_dp):
                    target[rows : 2 * rows, i * width : (i + 1) * width] = up_ref[
                        :, (4 * i + k) * width : (4 * i + k + 1) * width
                    ]

    for target in targets:
        start = 0
        for vector in vectors:
            width = vector.shape[0]
            target[2 * rows : 2 * rows + 1, start : start + width] = vector[...].reshape(1, width)
            start += width


def split_first(qkv_weight, out_weight, up_weight, vectors, quarter, n_dp):
    rows, model = out_weight.shape
    whole = pl.BlockSpec(memory_space=pltpu.VMEM)
    return pl.pallas_call(
        functools.partial(split_first_kernel, n_dp),
        in_specs=[pl.BlockSpec(memory_space=pltpu.SMEM)] + [whole] * (3 + len(vectors)),
        out_specs=[whole] * 2,
        out_shape=[jax.ShapeDtypeStruct((2 * rows + 8, model), BF16)] * 2,
        cost_estimate=pl.CostEstimate(
            flops=0, bytes_accessed=24 * rows * model, transcendentals=0
        ),
    )(quarter.reshape(1), qkv_weight, out_weight, up_weight, *vectors)


def split_rest_kernel(index_ref, down_ref, cell_ref, gene_ref, *targets):
    wide = cell_ref.shape[1] // 4
    cut = down_ref.shape[0] // 4
    for flip in range(2):
        down, decoder = targets[flip::2]
        start = pl.multiple_of((index_ref[0] ^ flip) * cut, cut)
        down[...] = down_ref[pl.ds(start, cut), :]
        for k in range(4):

            @pl.when(index_ref[0] == k ^ flip)
            def _():
                decoder[:, :wide] = cell_ref[:, k * wide : (k + 1) * wide]
                decoder[:, wide:] = gene_ref[:, k * wide : (k + 1) * wide]


def split_rest(down_weight, cell_weight, gene_weight, quarter):
    rows, wide = cell_weight.shape[0], cell_weight.shape[1] // 4
    whole = pl.BlockSpec(memory_space=pltpu.VMEM)
    shorter = jax.ShapeDtypeStruct((down_weight.shape[0] // 4, down_weight.shape[1]), BF16)
    return pl.pallas_call(
        split_rest_kernel,
        in_specs=[pl.BlockSpec(memory_space=pltpu.SMEM)] + [whole] * 3,
        out_specs=[whole] * 4,
        out_shape=[shorter] * 2 + [jax.ShapeDtypeStruct((rows, 2 * wide), BF16)] * 2,
        cost_estimate=pl.CostEstimate(
            flops=0, bytes_accessed=32 * rows * wide, transcendentals=0
        ),
        compiler_params=pltpu.CompilerParams(vmem_limit_bytes=32 << 20),
    )(quarter.reshape(1), down_weight, cell_weight, gene_weight)


def pack_kernel(room, index_ref, starts_ref, *refs):
    sources, out_ref = refs[:4], refs[4]
    micro, slots = sources[0].shape[0], sources[0].shape[1]
    for pair in range(2):
        for batch in range(micro):
            segment = (batch * 2 + pair) * room
            start = starts_ref[batch * 2 + pair]

            def put(first, second):
                kept = min(room, slots)
                out_ref[segment : segment + kept, :] = first[batch, 0:kept, :]

                def move(i, carry):
                    source = pl.multiple_of(jnp.minimum(i * 16, slots - 16), 16)
                    target = pl.multiple_of(segment + start + i * 16, 16)
                    out_ref[pl.ds(target, 16), :] = second[batch, pl.ds(source, 16), :]
                    return carry

                lax.fori_loop(0, (room - start) // 16, move, 0)

            pl.when(index_ref[1] == 0)(functools.partial(put, sources[2 * pair], sources[2 * pair + 1]))
            pl.when(index_ref[1] == 1)(functools.partial(put, sources[2 * pair + 1], sources[2 * pair]))


def pack(sources, index, starts, room):
    micro, _, model = sources[0].shape
    whole = pl.BlockSpec(memory_space=pltpu.VMEM)
    scalars = pl.BlockSpec(memory_space=pltpu.SMEM)
    return pl.pallas_call(
        functools.partial(pack_kernel, room),
        in_specs=[scalars, scalars] + [whole] * 4,
        out_specs=whole,
        out_shape=jax.ShapeDtypeStruct((2 * micro * room, model), BF16),
        cost_estimate=pl.CostEstimate(
            flops=0, bytes_accessed=12 * micro * room * model, transcendentals=0
        ),
        compiler_params=pltpu.CompilerParams(vmem_limit_bytes=40 << 20),
    )(index, starts, *sources)


def paste_kernel(index_ref, qkv_ref, *refs):
    blocks = [ref[...] for ref in refs[:4]]
    out_ref = refs[4]
    core, half = index_ref[0], index_ref[1]
    wide, part = qkv_ref.shape[1], blocks[0].shape[0]

    def swap(index, i, j):
        first = jnp.where(index == 0, blocks[i], blocks[j])
        blocks[j] = jnp.where(index == 0, blocks[j], blocks[i])
        blocks[i] = first

    swap(core, 0, 1)
    swap(core, 2, 3)
    swap(half, 0, 2)
    swap(half, 1, 3)
    out_ref[:, 0:wide] = qkv_ref[...]
    for i, block in enumerate(blocks):
        out_ref[i * part : (i + 1) * part, wide:] = block


def paste(grad_qkv, blocks, index):
    rows, wide = grad_qkv.shape
    whole = pl.BlockSpec(memory_space=pltpu.VMEM)
    return pl.pallas_call(
        paste_kernel,
        in_specs=[pl.BlockSpec(memory_space=pltpu.SMEM)] + [whole] * 5,
        out_specs=whole,
        out_shape=jax.ShapeDtypeStruct((rows, wide + blocks[0].shape[1]), BF16),
        cost_estimate=pl.CostEstimate(
            flops=0, bytes_accessed=6 * rows * wide, transcendentals=0
        ),
        compiler_params=pltpu.CompilerParams(vmem_limit_bytes=32 << 20),
    )(index, grad_qkv, *blocks)


def shards(
    n_dp,
    n_query,
    tokens,
    out_cotangent,
    qkv_weight,
    out_weight,
    up_weight,
    down_weight,
    attn_gain,
    ffn_gain,
    up_bias,
    cell_weight,
    gene_weight,
    decoder_bias,
    readout,
    gene_embed,
    query_cell,
    query_label,
    query_live,
):
    micro, _, length, model = tokens.shape
    slots = gene_embed.shape[2]
    chips = n_dp // 2
    shard = model // n_dp
    ff_shard = up_bias.shape[0]
    dh_shard = decoder_bias.shape[0]
    part = model // 4
    ff_part = ff_shard * n_dp // 4
    dh_part = dh_shard * n_dp // 4
    room = 2 * slots if n_query > 2 else (2 * slots * 5 // 8 + 15) // 16 * 16 + 16
    dp_index = lax.axis_index("dp").astype(jnp.int32)
    query_index = lax.axis_index("query").astype(jnp.int32)
    core = dp_index % 2
    half = query_index % 2
    quarter = 2 * half + core
    index = jnp.stack([core, half])
    chip = dp_index // 2
    position = jnp.where(chip % 2 == 0, chip // 2, chips - 1 - chip // 2)
    ring = [2 * i for i in range(chips // 2)] + [2 * i + 1 for i in reversed(range(chips // 2))]
    same_core = [[2 * i + k for i in range(chips)] for k in range(2)]
    chip_bits = [1 << i for i in range(1, n_dp.bit_length() - 1)]
    query_bits = [1 << i for i in range(n_query.bit_length() - 1)]

    def ring_moves(step):
        return [
            (2 * ring[i] + k, 2 * ring[(i + step) % chips] + k) for i in range(chips) for k in range(2)
        ]

    ahead, behind = ring_moves(1), ring_moves(-1)

    def dp_swap(value, bit):
        return lax.ppermute(value, "dp", [(i, i ^ bit) for i in range(n_dp)])

    def core_swap(value):
        return dp_swap(value, 1)

    def query_swap(value, bit=1):
        return lax.ppermute(value, "query", [(i, i ^ bit) for i in range(n_query)])

    def gather_four(value):
        near = jnp.stack([value, query_swap(value)], axis=1)
        return jnp.concatenate([near, core_swap(near)], axis=1)

    def scatter_four(value, batches):
        blocks = value.reshape((batches, 4, -1) + value.shape[1:])
        received = core_swap(blocks[:, 2:].astype(BF16))
        far = query_swap((blocks[:, 1] + received[:, 1].astype(F32)).astype(BF16))
        total = blocks[:, 0] + received[:, 0].astype(F32) + far.astype(F32)
        return total.reshape((-1,) + value.shape[1:])

    def order(which, first, second):
        return jnp.where(which == 0, first, second), jnp.where(which == 0, second, first)

    def by_quarter(a, b, c, d):
        a, b = order(core, a, b)
        c, d = order(core, c, d)
        a, c = order(half, a, c)
        b, d = order(half, b, d)
        return [a, b, c, d]

    def exchange_four(blocks):
        own, near, far, both = by_quarter(*blocks)
        theirs = core_swap(jnp.stack([near, both]))
        beyond = query_swap(jnp.stack([far, theirs[1]]))
        return own, theirs[0], beyond[0], beyond[1]

    def ring_start(mine, theirs):
        low, high = order(core, mine, core_swap(theirs))
        return [low, high]

    def last(held):
        return tuple(held[-2:])

    def pin(value, *events):
        return lax.optimization_barrier((value, *events))[0]

    def ring_step(held, *events):
        if len(held) < 2 * chips:
            low, high = lax.optimization_barrier((*last(held), *events))[:2]
            held.append(lax.ppermute(low, "dp", ahead))
            held.append(lax.ppermute(high, "dp", behind))

    def other_pairs(value):
        for bit in query_bits[1:]:
            value = value + query_swap(value, bit)
        return value

    def to_owner(low, high):
        mine, theirs = order(core, low, high)
        theirs = core_swap(theirs)
        far = query_swap(jnp.stack([mine, theirs]))
        return mine, theirs, far[0], far[1]

    def cores(rows):
        return rows[:shard], rows[shard:]

    def ring_scatter(grads):
        rows = grads.shape[0] // n_dp

        def piece(offset, side):
            start = (2 * ring_chip(position + offset, chips) + side) * rows
            return lax.dynamic_slice(grads, (start, 0), (rows, grads.shape[1]))

        low, high = piece(-1, 0), piece(1, 1)
        for step in range(1, chips):
            low = lax.ppermute(low, "dp", ahead)
            high = lax.ppermute(high, "dp", behind)
            low = (low.astype(F32) + piece(-1 - step, 0).astype(F32)).astype(BF16)
            high = (high.astype(F32) + piece(1 + step, 1).astype(F32)).astype(BF16)
        return other_pairs(low), other_pairs(high)

    def ring_scatter(grads):
        rows = grads.shape[0] // n_dp

        def piece(offset, side):
            start = (2 * ring_chip(position + offset, chips) + side) * rows
            return lax.dynamic_slice(grads, (start, 0), (rows, grads.shape[1]))

        low, high = piece(-1, 0), piece(1, 1)
        for step in range(1, chips):
            low = lax.ppermute(low, "dp", ahead)
            high = lax.ppermute(high, "dp", behind)
            low = (low.astype(F32) + piece(-1 - step, 0).astype(F32)).astype(BF16)
            high = (high.astype(F32) + piece(1 + step, 1).astype(F32)).astype(BF16)
        return other_pairs(low), other_pairs(high)

    def chip_rows(mine, theirs):
        return jnp.concatenate(order(core, mine, core_swap(theirs)))

    def plane_gather(rows):
        return lax.all_gather(rows, "dp", axis=0, tiled=True, axis_index_groups=same_core)

    def plane_scatter(grads):
        return lax.psum_scatter(
            grads, "dp", scatter_dimension=0, tiled=True, axis_index_groups=same_core
        )

    def group_sum(values):
        values = values + core_swap(values)[:, ::-1]
        return values + query_swap(values)

    first_ring = ring_start(
        *split_first(
            qkv_weight,
            out_weight,
            up_weight,
            [attn_gain, ffn_gain, up_bias, decoder_bias, readout],
            quarter,
            n_dp,
        )
    )
    down_mine, down_theirs, decoder_mine, decoder_theirs = split_rest(
        down_weight, cell_weight, gene_weight, quarter
    )
    tokens_far = query_swap(tokens[:, 0])
    cotangent_far = query_swap(pin(out_cotangent, tokens_far)[:, 0])
    gene_far = query_swap(pin(gene_embed, tokens_far)[:, 0])

    def with_cores(own, far):
        near = jnp.stack([own, far], axis=1)
        return jnp.concatenate([near, core_swap(near)], axis=1).reshape(-1, model)

    live = jnp.arange(slots, dtype=jnp.int32)[None, :] < query_live[0, :, 0][:, None]
    facts = jnp.stack(
        [query_cell[:, 0].astype(F32), query_label[:, 0].astype(F32), live.astype(F32)], axis=1
    ).reshape(micro * 3, slots)
    facts = jnp.concatenate(
        [facts, jnp.broadcast_to(query_live[0, :, 0].astype(F32)[:, None], (micro, slots))]
    )
    facts = jnp.stack(order(half, facts, query_swap(facts)), axis=1)
    facts = jnp.stack([facts, core_swap(facts)], axis=1)
    starts = (facts[3 * micro :, :, 0, 0].astype(jnp.int32) + 15) // 16 * 16
    facts = facts[: 3 * micro].reshape(micro, 3, 2, 2, slots)
    packed = []
    for batch in range(micro):
        for pair in range(2):
            line = jnp.pad(facts[batch, :, pair, 0], ((0, 0), (0, room)))
            line = lax.dynamic_update_slice(line, facts[batch, :, pair, 1], (0, starts[batch, pair]))
            packed.append(line[:, :room])
    facts = jnp.stack(packed, axis=1).reshape(3, micro, 2, room)
    starts = starts.reshape(-1)
    own_tokens = tokens[:, 0].reshape(micro * length, model)
    for step in range(1, chips):
        arrived = {3: (tokens_far,), chips - 2: (cotangent_far,), chips - 1: (gene_far,)}.get(step, ())
        ring_step(first_ring, *arrived)
        if step == chips - 2:
            down_rows = pin(chip_rows(down_mine, down_theirs), *first_ring[-4:-2])
            decoder_rows = pin(chip_rows(decoder_mine, decoder_theirs), *first_ring[-4:-2])
            down_part, decoder_part = plane_gather(down_rows), plane_gather(decoder_rows)
        if step == 3:
            all_tokens = with_cores(tokens[:, 0], tokens_far)
            norm_all, _ = layer_stats(all_tokens.astype(F32))
    attention_part, up_part, vectors = place(first_ring, position, (shard, shard, 8))
    all_cotangent = with_cores(out_cotangent[:, 0], cotangent_far)

    vectors = vectors.reshape(n_dp, 8, model)[:, 0].astype(F32)
    bounds = [0, shard, 2 * shard, 2 * shard + ff_shard, 2 * shard + ff_shard + dh_shard]
    bounds.append(bounds[-1] + dh_shard)
    pieces = [vectors[:, low:high] for low, high in zip(bounds[:-1], bounds[1:])]
    attn_gain_all = pieces[0].reshape(model)
    ffn_gain_all = pieces[1].reshape(model)
    up_bias_part = lax.dynamic_index_in_dim(
        pieces[2].reshape(n_dp, 4, ff_shard // 4), quarter, 1, keepdims=False
    ).reshape(ff_part)
    decoder_bias_part = lax.dynamic_slice(pieces[3].reshape(-1), (quarter * dh_part,), (dh_part,))
    readout_part = lax.dynamic_slice(pieces[4].reshape(-1), (quarter * dh_part,), (dh_part,))
    qkv_part = attention_part[:, : 3 * part]
    out_blocks = attention_part[:, 3 * part :].reshape(4, part, part)
    out_part = jnp.concatenate(
        by_quarter(*exchange_four([out_blocks[i] for i in range(4)])), axis=1
    )

    normed = (norm_all * attn_gain_all).astype(BF16)
    projected = product(pin(normed, all_cotangent), qkv_part).astype(BF16)
    own_wide = own_tokens.astype(F32)
    mixed, second, hidden, norm_two, scale_two = [], [], [], [], []
    for batch in range(micro):
        mixed.append(attend(projected, length, 4 * batch, 4))
        partial = product(mixed[-1], out_part)
        projected = pin(projected, partial)
        hidden.append(own_wide[batch * length : (batch + 1) * length] + scatter_four(partial, 1))
    gene_far = pin(gene_far, partial)
    gene_rows = pack(
        [gene_embed[:, 0], gene_far, core_swap(gene_embed[:, 0]), core_swap(gene_far)], index, starts, room
    )
    for batch in range(micro):
        normal, scale = layer_stats(hidden[batch])
        norm_two.append(normal)
        scale_two.append(scale)
        second.append(gather_four((normal * ffn_gain_all).astype(BF16)[None]))
    hidden, norm_two, scale_two = (jnp.concatenate(parts) for parts in (hidden, norm_two, scale_two))
    second = jnp.concatenate(second).reshape(-1, model)
    mixed = jnp.concatenate(mixed)
    up_proj = product(pin(second, gene_rows), up_part) + up_bias_part
    active = jax.nn.gelu(up_proj, approximate=True).astype(BF16)
    branch = product(active, down_part)

    def first_of(rows):
        return rows.reshape((-1, length) + rows.shape[1:])[:, 0]

    first_output = first_of(hidden) + scatter_four(first_of(branch), micro)
    output = (hidden + scatter_four(branch, micro)).reshape(micro, length, model)
    block_out = output.astype(BF16).at[:, 0].set(first_output.astype(BF16))

    gelu_back = jax.vjp(lambda inner: jax.nn.gelu(inner, approximate=True), up_proj)[1]
    grad_down_part = row_product(pin(active, branch), all_cotangent).astype(BF16)
    down_total = plane_scatter(grad_down_part)
    cotangent_in = pin(all_cotangent, grad_down_part)
    grad_up_proj = gelu_back(times_transpose(cotangent_in, down_part))[0].astype(BF16)
    grad_up_part = row_product(second, grad_up_proj).astype(BF16)
    up_total = plane_scatter(grad_up_part)
    grad_second = times_transpose(pin(grad_up_proj, grad_up_part), up_part)
    grad_second = scatter_four(grad_second, micro)
    cell_part, gene_part = decoder_part[:, :dh_part], decoder_part[:, dh_part:]
    grad_hidden_norm, _ = norm_back(grad_second, ffn_gain_all, norm_two, scale_two)
    own_cotangent = out_cotangent[:, 0].reshape(micro * length, model).astype(F32)
    grad_hidden = own_cotangent + grad_hidden_norm

    summaries = first_output.astype(BF16)
    for bit in query_bits:
        summaries = jnp.stack([summaries, query_swap(summaries, bit)])
    summaries = jnp.stack([summaries, core_swap(summaries)])
    cells = 2 * n_query * micro
    summaries = summaries.reshape(cells, model)
    cell_values = product(summaries, cell_part)
    cell_values = cell_values.reshape(2, n_query, micro, dh_part).transpose(2, 0, 1, 3)
    asked = facts[0].astype(jnp.int32) ^ query_index
    chosen_cell = cell_values[:, :, 0, None]
    for i in range(1, n_query):
        chosen_cell = jnp.where(asked[..., None] == i, cell_values[:, :, i, None], chosen_cell)
    asked = (jnp.arange(2)[None, :, None] * n_query + asked) * micro + jnp.arange(micro)[:, None, None]
    onehot = (asked.reshape(-1, 1) == jnp.arange(cells, dtype=jnp.int32)).astype(BF16)
    pre_act = product(gene_rows, gene_part).reshape(micro, 2, room, dh_part) + chosen_cell
    pre_act = pre_act + decoder_bias_part
    chance = jax.nn.sigmoid(pre_act)
    activity = pre_act * chance
    logits = jnp.sum(activity * readout_part, axis=-1)
    grad_hidden = pin(grad_hidden, logits)
    grad_attn = gather_four(grad_hidden.astype(BF16).reshape(micro, length, model)).reshape(-1, model)
    logits = group_sum(logits)
    grad_logits = facts[2] * (jax.nn.sigmoid(logits) - facts[1])
    grad_readout = jnp.sum(grad_logits[..., None] * activity, axis=(0, 1, 2))
    slope = chance * (1.0 + pre_act * (1.0 - chance))
    grad_pre = (grad_logits[..., None] * readout_part * slope).astype(BF16).reshape(-1, dh_part)
    grad_decoder_bias = jnp.sum(grad_pre.astype(F32), axis=0)
    grad_cells = row_product(onehot, grad_pre).astype(BF16)
    grad_gene_part = row_product(gene_rows, pin(grad_pre, grad_cells)).astype(BF16)
    gene_total = plane_scatter(grad_gene_part)
    grad_mixed = times_transpose(grad_attn, out_part).astype(BF16)

    grad_summary = times_transpose(grad_cells, cell_part).reshape(2, n_query, micro, model)
    grad_summary = grad_summary[0] + core_swap(grad_summary[1].astype(BF16)).astype(F32)
    for bit in reversed(query_bits):
        grad_summary = grad_summary.reshape(2, -1, micro, model)
        far = query_swap(grad_summary[1].astype(BF16), bit)
        grad_summary = grad_summary[0] + far.astype(F32)
    grad_summary = grad_summary.reshape(micro, model)

    first_cotangent = first_of(own_cotangent)
    first_grad = first_cotangent + grad_summary
    first_branch = gather_four(first_grad.astype(BF16)[:, None]).reshape(-1, model)
    first_change = (first_branch.astype(F32) - first_of(all_cotangent).astype(F32)).astype(BF16)
    first_gelu_back = jax.vjp(
        lambda inner: jax.nn.gelu(inner, approximate=True), first_of(up_proj)
    )[1]
    first_up = first_gelu_back(times_transpose(first_branch, down_part))[0].astype(BF16)
    first_up_change = (first_up.astype(F32) - first_of(grad_up_proj).astype(F32)).astype(BF16)
    first_second = scatter_four(times_transpose(first_up, up_part), micro)
    first_norm, first_scale = first_of(norm_two), first_of(scale_two)
    first_hidden, first_gain = norm_back(first_second, ffn_gain_all, first_norm, first_scale)
    first_hidden = first_grad + first_hidden
    first_attn = gather_four(first_hidden.astype(BF16)[:, None]).reshape(-1, model)
    first_mixed = times_transpose(first_attn, out_part).astype(BF16)
    first_attn_change = (first_attn.astype(F32) - first_of(grad_attn).astype(F32)).astype(BF16)
    grad_up_bias = jnp.sum(grad_up_proj.astype(F32), axis=0) + jnp.sum(
        first_up_change.astype(F32), axis=0
    )
    is_first = jnp.arange(micro * length)[:, None] % length == 0
    grad_ffn_gain = first_gain + jnp.sum(jnp.where(is_first, 0.0, grad_second * norm_two), axis=0)
    grad_hidden = grad_hidden.reshape(micro, length, model).at[:, 0].set(first_hidden)
    grad_hidden = grad_hidden.reshape(micro * length, model)

    left = jnp.concatenate([first_of(active), first_of(second), summaries])[None]
    right = jnp.concatenate([first_change, first_up_change, grad_cells])[None]
    for bit in chip_bits:
        left = jnp.concatenate([left, dp_swap(left, bit)])
        right = jnp.concatenate([right, dp_swap(right, bit)])
    left = left.reshape(chips, left.shape[1], chips, 2 * shard)
    left = lax.dynamic_index_in_dim(left, chip, 2, keepdims=False)

    def few_rows(start, stop):
        return row_product(
            left[:, start:stop].reshape(-1, 2 * shard), right[:, start:stop].reshape(-1, ff_part)
        )

    firsts = 4 * micro
    grad_down_rows = few_rows(0, firsts)
    grad_up_rows = few_rows(firsts, 2 * firsts)
    grad_cell_rows = few_rows(2 * firsts, 2 * firsts + cells)

    grad_out_part = row_product(mixed, grad_attn) + row_product(first_of(mixed), first_attn_change)
    grad_out_part = grad_out_part.astype(BF16)
    out_blocks = exchange_four([grad_out_part[:, i * part : (i + 1) * part] for i in range(4)])
    few = jnp.stack([down_total, up_total, jnp.zeros_like(up_total)]).astype(F32)
    few = few + jnp.stack([grad_down_rows, grad_up_rows, grad_cell_rows])
    few = other_pairs(few.astype(BF16)).reshape(3, 2, shard, model)
    few_owned = to_owner(few[:, 0], few[:, 1])
    gene_owned = to_owner(*cores(other_pairs(gene_total)))
    grad_projected = attend_back(projected, grad_mixed, first_mixed[:, None], length)
    grad_projected = pin(grad_projected, *few_owned)
    grad_qkv_part = row_product(normed, grad_projected).astype(BF16)
    attention_grads = ring_scatter(paste(grad_qkv_part, out_blocks, index))
    grad_normed = times_transpose(pin(grad_projected, grad_qkv_part), qkv_part)
    grad_normed = scatter_four(grad_normed, micro)
    norm_one, scale_one = layer_stats(own_wide)
    grad_input_norm, grad_attn_gain = norm_back(grad_normed, attn_gain_all, norm_one, scale_one)
    grad_tokens = (grad_hidden + grad_input_norm).reshape(micro, 1, length, model)

    grad_gene = jnp.concatenate(by_quarter(*gene_owned), axis=1).astype(F32)
    down_rows, up_rows, cell_rows = zip(*((block[0], block[1], block[2]) for block in few_owned))
    grad_cell = jnp.concatenate(by_quarter(*cell_rows), axis=1).astype(F32)
    grad_down = jnp.concatenate(by_quarter(*down_rows)).astype(F32)
    (grad_up,) = join(up_rows, index, column_places("up", ff_part, n_dp), [4 * ff_part])
    grad_qkv, grad_out = join(
        to_owner(*attention_grads), index, column_places("attention", part, n_dp), [3 * model, model]
    )

    chosen = (jnp.arange(4) == quarter).astype(F32)
    owned = jnp.concatenate(
        [
            grad_attn_gain.reshape(n_dp, shard),
            grad_ffn_gain.reshape(n_dp, shard),
            (grad_up_bias.reshape(n_dp, 1, ff_shard // 4) * chosen[:, None]).reshape(n_dp, ff_shard),
            (chosen[:, None] * grad_decoder_bias).reshape(n_dp, dh_shard),
            (chosen[:, None] * grad_readout).reshape(n_dp, dh_shard),
        ],
        axis=1,
    )
    for bit in reversed([1] + chip_bits):
        owned = owned.reshape((2, owned.shape[0] // 2) + owned.shape[1:])
        kept, sent = order((dp_index // bit) % 2, owned[0], owned[1])
        owned = kept + dp_swap(sent, bit)
    for bit in query_bits:
        owned = owned + query_swap(owned, bit)
    small = [owned[0, low:high] for low, high in zip(bounds[:-1], bounds[1:])]
    return (
        block_out[:, None],
        grad_tokens,
        grad_qkv,
        grad_out,
        grad_up,
        grad_down,
        small[0],
        small[1],
        small[2],
        grad_cell,
        grad_gene,
        small[3],
        small[4],
    )


def solution(mesh):
    cells = P(None, ("dp", "query"), None, None)
    rows = P("dp", None)
    vector = P("dp")
    slots = P(None, ("dp", "query"), None)
    return jax.shard_map(
        functools.partial(shards, mesh.shape["dp"], mesh.shape["query"]),
        mesh=mesh,
        in_specs=(
            cells, cells, rows, rows, rows, rows, vector, vector, vector, rows, rows, vector, vector,
            cells, slots, slots, P("dp", None, "query"),
        ),
        out_specs=(
            cells, cells, rows, rows, rows, rows, vector, vector, vector, rows, rows, vector, vector,
        ),
        check_vma=False,
    )
```

```python
import functools

import jax
import jax.numpy as jnp
from jax import lax
from jax.experimental import pallas as pl
from jax.experimental.pallas import tpu as pltpu
from jax.sharding import PartitionSpec as P

HEAD = 64
EPSILON = 1e-05
F32 = jnp.float32
BF16 = jnp.bfloat16


def product(left, right):
    return jnp.dot(left, right, preferred_element_type=F32)


def row_product(left, right):
    return lax.dot_general(left, right, (((0,), (0,)), ((), ())), preferred_element_type=F32)


def times_transpose(left, right):
    return lax.dot_general(left, right, (((1,), (1,)), ((), ())), preferred_element_type=F32)


def layer_stats(values):
    average = jnp.mean(values, axis=-1, keepdims=True)
    centred = values - average
    variance = jnp.mean(centred * centred, axis=-1, keepdims=True)
    inverse = lax.rsqrt(variance + EPSILON)
    return (centred * inverse, inverse)


def norm_back(grad_scaled, gain, normal, inverse):
    grad_normal = grad_scaled * gain
    along_normal = jnp.mean(grad_normal * normal, axis=-1, keepdims=True)
    average = jnp.mean(grad_normal, axis=-1, keepdims=True)
    grad_values = inverse * (grad_normal - average - normal * along_normal)
    return (grad_values, jnp.sum(grad_scaled * normal, axis=0))


def norm_kernel(gain_ref, *refs):
    sources, out_ref = refs[:-1], refs[-1]
    micro, length, _ = sources[0].shape
    for batch in range(micro):
        for i, source in enumerate(sources):
            normal, _ = layer_stats(source[batch].astype(F32))
            start = (batch * len(sources) + i) * length
            out_ref[start : start + length, :] = (normal * gain_ref[...]).astype(BF16)


def norm_four(sources, gain):
    micro, length, model = sources[0].shape
    rows = len(sources) * micro * length
    whole = pl.BlockSpec(memory_space=pltpu.VMEM)
    return pl.pallas_call(
        norm_kernel,
        in_specs=[whole] * (1 + len(sources)),
        out_specs=whole,
        out_shape=jax.ShapeDtypeStruct((rows, model), BF16),
        cost_estimate=pl.CostEstimate(
            flops=8 * rows * model, bytes_accessed=4 * rows * model, transcendentals=rows
        ),
        compiler_params=pltpu.CompilerParams(vmem_limit_bytes=32 << 20),
    )(gain[None], *sources)


def softmax_all(scores):
    shifted = [jnp.exp(value - jnp.max(value, axis=-1, keepdims=True)) for value in scores]
    return [value * (1.0 / jnp.sum(value, axis=-1, keepdims=True)) for value in shifted]


def heads_of(ref, width, part):
    return [ref[:, part * width + i : part * width + i + HEAD] for i in range(0, width, HEAD)]


def attend_kernel(projected_ref, mixed_ref):
    width = mixed_ref.shape[1]
    queries, keys, values = (heads_of(projected_ref, width, part) for part in range(3))
    probs = softmax_all([times_transpose(q, k) * 0.125 for q, k in zip(queries, keys)])
    mixed = [product(p.astype(BF16), v).astype(BF16) for p, v in zip(probs, values)]
    for i, value in enumerate(mixed):
        mixed_ref[:, i * HEAD : (i + 1) * HEAD] = value


def attend_back_kernel(projected_ref, grad_mixed_ref, first_ref, grad_ref):
    width = grad_mixed_ref.shape[1]
    is_first = lax.broadcasted_iota(jnp.int32, (grad_mixed_ref.shape[0], width), 0) == 0
    grad_ref[:, 0:width] = jnp.where(is_first, first_ref[0], grad_mixed_ref[...])
    grads = heads_of(grad_ref, width, 0)
    queries, keys, values = (heads_of(projected_ref, width, part) for part in range(3))
    scores = [times_transpose(q, k) * 0.125 for q, k in zip(queries, keys)]
    grad_probs = [times_transpose(g, v) for g, v in zip(grads, values)]
    probs = softmax_all(scores)
    grad_values = [row_product(p.astype(BF16), g) for p, g in zip(probs, grads)]
    along = [jnp.sum(g * p, axis=-1, keepdims=True) for g, p in zip(grad_probs, probs)]
    grad_scores = [
        (p * (g - a) * 0.125).astype(BF16) for p, g, a in zip(probs, grad_probs, along)
    ]
    grad_queries = [product(g, k) for g, k in zip(grad_scores, keys)]
    grad_keys = [row_product(g, q) for g, q in zip(grad_scores, queries)]
    for part, parts in enumerate((grad_queries, grad_keys, grad_values)):
        for i, value in enumerate(parts):
            start = part * width + i * HEAD
            grad_ref[:, start : start + HEAD] = value.astype(BF16)


def attend(projected, length, first, count):
    rows, wide = count * length, projected.shape[1]
    return pl.pallas_call(
        attend_kernel,
        grid=(count,),
        in_specs=[pl.BlockSpec((length, wide), lambda i: (first + i, 0))],
        out_specs=pl.BlockSpec((length, wide // 3), lambda i: (i, 0)),
        out_shape=jax.ShapeDtypeStruct((rows, wide // 3), BF16),
        cost_estimate=pl.CostEstimate(
            flops=4 * rows * length * wide // 3,
            bytes_accessed=rows * wide * 3,
            transcendentals=rows * length * wide // 3 // HEAD,
        ),
    )(projected)


def attend_back(projected, grad_mixed, first, length):
    rows, wide = projected.shape
    return pl.pallas_call(
        attend_back_kernel,
        grid=(rows // length,),
        in_specs=[
            pl.BlockSpec((length, wide), lambda i: (i, 0)),
            pl.BlockSpec((length, wide // 3), lambda i: (i, 0)),
            pl.BlockSpec((1, 1, wide // 3), lambda i: (i, 0, 0)),
        ],
        out_specs=pl.BlockSpec((length, wide), lambda i: (i, 0)),
        out_shape=jax.ShapeDtypeStruct((rows, wide), BF16),
        cost_estimate=pl.CostEstimate(
            flops=10 * rows * length * wide // 3,
            bytes_accessed=rows * wide * 5,
            transcendentals=rows * length * wide // 3 // HEAD,
        ),
    )(projected, grad_mixed, first)


def ring_chip(position, chips):
    position = lax.rem(position + 2 * chips, chips)
    return jnp.where(position < chips // 2, 2 * position, 2 * (chips - 1 - position) + 1)


def place_kernel(segments, position_ref, *refs):
    outs, sems = refs[-1 - len(segments) : -1], refs[-1]
    count = (len(refs) - 1 - len(segments)) // 2
    copies = []
    for step in range(count):
        for side in range(2):
            piece = refs[2 * step + side]
            source = ring_chip(position_ref[0] + (step if side else -step), count)
            begin = 0
            for out, rows in zip(outs, segments):
                start = pl.multiple_of((2 * source + side) * rows, rows)
                copies.append(
                    pltpu.make_async_copy(
                        piece.at[pl.ds(begin, rows), :], out.at[pl.ds(start, rows), :], sems.at[len(copies)]
                    )
                )
                begin += rows
    for copy in copies:
        copy.start()
    for copy in copies:
        copy.wait()


def place(pieces, position, segments):
    tall, wide = pieces[0].shape
    whole = pl.BlockSpec(memory_space=pltpu.VMEM)
    return pl.pallas_call(
        functools.partial(place_kernel, segments),
        in_specs=[pl.BlockSpec(memory_space=pltpu.SMEM)]
        + [pl.BlockSpec(memory_space=pl.ANY)] * len(pieces),
        out_specs=[whole] * len(segments),
        scratch_shapes=[pltpu.SemaphoreType.DMA((len(pieces) * len(segments),))],
        out_shape=[jax.ShapeDtypeStruct((len(pieces) * rows, wide), BF16) for rows in segments],
        cost_estimate=pl.CostEstimate(
            flops=0, bytes_accessed=4 * len(pieces) * tall * wide, transcendentals=0
        ),
        compiler_params=pltpu.CompilerParams(vmem_limit_bytes=32 << 20),
    )(position.reshape(1), *pieces)


def column_places(kind, part, n_dp):
    if kind == "attention":
        model = 4 * part
        return [
            [(0, i * model + k * part, i * part, part) for i in range(3)] + [(1, k * part, 3 * part, part)]
            for k in range(4)
        ]
    width = part // n_dp
    return [[(0, (4 * i + k) * width, i * width, width) for i in range(n_dp)] for k in range(4)]


def join_kernel(places, index_ref, *refs):
    blocks = [ref[...].astype(F32) for ref in refs[:4]]
    core, half = index_ref[0], index_ref[1]

    def swap(index, i, j):
        first = jnp.where(index == 0, blocks[i], blocks[j])
        blocks[j] = jnp.where(index == 0, blocks[j], blocks[i])
        blocks[i] = first

    swap(core, 0, 1)
    swap(core, 2, 3)
    swap(half, 0, 2)
    swap(half, 1, 3)
    for block, moves in zip(blocks, places):
        for output, start, source, width in moves:
            refs[4 + output][:, start : start + width] = block[:, source : source + width]


def join(blocks, index, places, widths):
    rows = blocks[0].shape[0]
    whole = pl.BlockSpec(memory_space=pltpu.VMEM)
    return pl.pallas_call(
        functools.partial(join_kernel, places),
        in_specs=[pl.BlockSpec(memory_space=pltpu.SMEM)] + [whole] * 4,
        out_specs=[whole] * len(widths),
        out_shape=[jax.ShapeDtypeStruct((rows, width), F32) for width in widths],
        cost_estimate=pl.CostEstimate(
            flops=0, bytes_accessed=6 * rows * sum(widths), transcendentals=0
        ),
        compiler_params=pltpu.CompilerParams(vmem_limit_bytes=32 << 20),
    )(index, *blocks)


def split_attention_kernel(index_ref, qkv_ref, out_ref, *refs):
    vectors, targets = refs[:-2], refs[-2:]
    rows, part = out_ref.shape[0], out_ref.shape[1] // 4
    for k in range(4):
        for flip, target in enumerate(targets):

            @pl.when(index_ref[0] == k ^ flip)
            def _():
                for i in range(3):
                    target[0:rows, i * part : (i + 1) * part] = qkv_ref[
                        :, (4 * i + k) * part : (4 * i + k + 1) * part
                    ]
                target[0:rows, 3 * part :] = out_ref[:, k * part : (k + 1) * part]

    for target in targets:
        start = 0
        for vector in vectors:
            width = vector.shape[0]
            target[rows : rows + 1, start : start + width] = vector[...].reshape(1, width)
            start += width


def split_attention(qkv_weight, out_weight, vectors, quarter):
    rows, model = out_weight.shape
    whole = pl.BlockSpec(memory_space=pltpu.VMEM)
    return pl.pallas_call(
        split_attention_kernel,
        in_specs=[pl.BlockSpec(memory_space=pltpu.SMEM)] + [whole] * (2 + len(vectors)),
        out_specs=[whole] * 2,
        out_shape=[jax.ShapeDtypeStruct((rows + 8, model), BF16)] * 2,
        cost_estimate=pl.CostEstimate(
            flops=0, bytes_accessed=12 * rows * model, transcendentals=0
        ),
    )(quarter.reshape(1), qkv_weight, out_weight, *vectors)


def split_rest_kernel(n_dp, index_ref, up_ref, down_ref, cell_ref, gene_ref, *targets):
    wide = cell_ref.shape[1] // 4
    cut = down_ref.shape[0] // 4
    width = wide // n_dp
    for flip in range(2):
        up, down, decoder = targets[flip::2]
        start = pl.multiple_of((index_ref[0] ^ flip) * cut, cut)
        down[...] = down_ref[pl.ds(start, cut), :]
        for k in range(4):

            @pl.when(index_ref[0] == k ^ flip)
            def _():
                for i in range(n_dp):
                    up[:, i * width : (i + 1) * width] = up_ref[
                        :, (4 * i + k) * width : (4 * i + k + 1) * width
                    ]
                decoder[:, :wide] = cell_ref[:, k * wide : (k + 1) * wide]
                decoder[:, wide:] = gene_ref[:, k * wide : (k + 1) * wide]


def split_rest(up_weight, down_weight, cell_weight, gene_weight, quarter, n_dp):
    rows, wide = cell_weight.shape[0], cell_weight.shape[1] // 4
    whole = pl.BlockSpec(memory_space=pltpu.VMEM)
    narrow = jax.ShapeDtypeStruct((rows, wide), BF16)
    shorter = jax.ShapeDtypeStruct((down_weight.shape[0] // 4, down_weight.shape[1]), BF16)
    return pl.pallas_call(
        functools.partial(split_rest_kernel, n_dp),
        in_specs=[pl.BlockSpec(memory_space=pltpu.SMEM)] + [whole] * 4,
        out_specs=[whole] * 6,
        out_shape=[narrow] * 2 + [shorter] * 2 + [jax.ShapeDtypeStruct((rows, 2 * wide), BF16)] * 2,
        cost_estimate=pl.CostEstimate(
            flops=0, bytes_accessed=40 * rows * wide, transcendentals=0
        ),
        compiler_params=pltpu.CompilerParams(vmem_limit_bytes=32 << 20),
    )(quarter.reshape(1), up_weight, down_weight, cell_weight, gene_weight)


def first_kernel(*refs):
    count = len(refs) // 2
    for source, target in zip(refs[:count], refs[count:]):
        for i in range(source.shape[0]):
            target[i : i + 1, :] = source[i, 0:1, :]


def first_rows_of(values, length):
    cells = values[0].shape[0] // length
    values = [value.reshape(cells, length, value.shape[1]) for value in values]
    specs = [pl.BlockSpec((cells, 16, value.shape[2]), lambda i: (0, 0, 0)) for value in values]
    outs = [pl.BlockSpec((cells, value.shape[2]), lambda i: (0, 0)) for value in values]
    return pl.pallas_call(
        first_kernel,
        grid=(1,),
        in_specs=specs,
        out_specs=outs,
        out_shape=[jax.ShapeDtypeStruct((cells, value.shape[2]), value.dtype) for value in values],
        cost_estimate=pl.CostEstimate(
            flops=0, bytes_accessed=64 * cells * sum(value.shape[2] for value in values), transcendentals=0
        ),
    )(*values)


def pack_kernel(room, index_ref, starts_ref, *refs):
    sources, out_ref = refs[:-1], refs[-1]
    micro = len(sources) // 4
    slots = sources[0].shape[0]
    for pair in range(2):
        for batch in range(micro):
            segment = (batch * 2 + pair) * room
            start = starts_ref[batch * 2 + pair]

            def put(first, second):
                kept = min(room, slots)
                out_ref[segment : segment + kept, :] = first[0:kept, :]

                def move(i, carry):
                    source = pl.multiple_of(jnp.minimum(i * 16, slots - 16), 16)
                    target = pl.multiple_of(segment + start + i * 16, 16)
                    out_ref[pl.ds(target, 16), :] = second[pl.ds(source, 16), :]
                    return carry

                lax.fori_loop(0, (room - start) // 16, move, 0)

            own = sources[2 * pair * micro + batch]
            far = sources[(2 * pair + 1) * micro + batch]
            pl.when(index_ref[1] == 0)(functools.partial(put, own, far))
            pl.when(index_ref[1] == 1)(functools.partial(put, far, own))


def pack(sources, index, starts, room):
    model = sources[0].shape[1]
    whole = pl.BlockSpec(memory_space=pltpu.VMEM)
    scalars = pl.BlockSpec(memory_space=pltpu.SMEM)
    total = len(sources) // 2 * room
    return pl.pallas_call(
        functools.partial(pack_kernel, room),
        in_specs=[scalars, scalars] + [whole] * len(sources),
        out_specs=whole,
        out_shape=jax.ShapeDtypeStruct((total, model), BF16),
        cost_estimate=pl.CostEstimate(flops=0, bytes_accessed=5 * total * model, transcendentals=0),
        compiler_params=pltpu.CompilerParams(vmem_limit_bytes=40 << 20),
    )(index, starts, *sources)


def facts_kernel(live_ref, cell_ref, label_ref, out_ref):
    micro, slots = cell_ref.shape
    lane = lax.broadcasted_iota(jnp.int32, (1, slots), 1)
    for batch in range(micro):
        out_ref[batch, 0:1, :] = cell_ref[batch : batch + 1, :].astype(F32)
        out_ref[batch, 1:2, :] = label_ref[batch : batch + 1, :].astype(F32)
        out_ref[batch, 2:3, :] = (lane < live_ref[batch]).astype(F32)
        out_ref[batch, 3:8, :] = jnp.full((5, slots), live_ref[batch], jnp.int32).astype(F32)


def facts_of(live, cell, label):
    whole = pl.BlockSpec(memory_space=pltpu.VMEM)
    return pl.pallas_call(
        facts_kernel,
        in_specs=[pl.BlockSpec(memory_space=pltpu.SMEM)] + [whole] * 2,
        out_specs=whole,
        out_shape=jax.ShapeDtypeStruct((cell.shape[0], 8, cell.shape[1]), F32),
        cost_estimate=pl.CostEstimate(flops=0, bytes_accessed=40 * cell.size, transcendentals=0),
    )(live, cell, label)


def line_kernel(index_ref, starts_ref, *refs):
    sources, out_ref = refs[:4], refs[4]
    micro, facts, slots = sources[0].shape
    room = out_ref.shape[3]
    wide = -(-(room + slots) // 128) * 128
    lane = lax.broadcasted_iota(jnp.int32, (facts, wide), 1)
    beyond = jnp.zeros((facts, wide - slots), F32)
    for batch in range(micro):
        for pair in range(2):
            own, far = sources[2 * pair][batch], sources[2 * pair + 1][batch]
            first = jnp.where(index_ref[1] == 0, own, far)
            second = jnp.where(index_ref[1] == 0, far, own)
            start = starts_ref[2 * batch + pair]
            moved = pltpu.roll(jnp.concatenate([second, beyond], axis=1), start, 1)
            line = jnp.where(lane < start, jnp.concatenate([first, beyond], axis=1), moved)
            out_ref[batch, pair] = line[:, :room]


def line_up(sources, index, starts, room):
    micro, facts, slots = sources[0].shape
    whole = pl.BlockSpec(memory_space=pltpu.VMEM)
    scalars = pl.BlockSpec(memory_space=pltpu.SMEM)
    return pl.pallas_call(
        functools.partial(line_kernel),
        in_specs=[scalars, scalars] + [whole] * 4,
        out_specs=whole,
        out_shape=jax.ShapeDtypeStruct((micro, 2, facts, room), F32),
        cost_estimate=pl.CostEstimate(
            flops=0, bytes_accessed=64 * micro * facts * slots, transcendentals=0
        ),
    )(index, starts, *sources)


def paste_kernel(index_ref, qkv_ref, *refs):
    blocks = [ref[...] for ref in refs[:4]]
    out_ref = refs[4]
    core, half = index_ref[0], index_ref[1]
    wide, part = qkv_ref.shape[1], blocks[0].shape[0]

    def swap(index, i, j):
        first = jnp.where(index == 0, blocks[i], blocks[j])
        blocks[j] = jnp.where(index == 0, blocks[j], blocks[i])
        blocks[i] = first

    swap(core, 0, 1)
    swap(core, 2, 3)
    swap(half, 0, 2)
    swap(half, 1, 3)
    out_ref[:, 0:wide] = qkv_ref[...]
    for i, block in enumerate(blocks):
        out_ref[i * part : (i + 1) * part, wide:] = block


def paste(grad_qkv, blocks, index):
    rows, wide = grad_qkv.shape
    whole = pl.BlockSpec(memory_space=pltpu.VMEM)
    return pl.pallas_call(
        paste_kernel,
        in_specs=[pl.BlockSpec(memory_space=pltpu.SMEM)] + [whole] * 5,
        out_specs=whole,
        out_shape=jax.ShapeDtypeStruct((rows, wide + blocks[0].shape[1]), BF16),
        cost_estimate=pl.CostEstimate(
            flops=0, bytes_accessed=6 * rows * wide, transcendentals=0
        ),
        compiler_params=pltpu.CompilerParams(vmem_limit_bytes=32 << 20),
    )(index, grad_qkv, *blocks)


def shards(
    n_dp,
    n_query,
    tokens,
    out_cotangent,
    qkv_weight,
    out_weight,
    up_weight,
    down_weight,
    attn_gain,
    ffn_gain,
    up_bias,
    cell_weight,
    gene_weight,
    decoder_bias,
    readout,
    gene_embed,
    query_cell,
    query_label,
    query_live,
):
    micro, _, length, model = tokens.shape
    slots = gene_embed.shape[2]
    chips = n_dp // 2
    shard = model // n_dp
    ff_shard = up_bias.shape[0]
    dh_shard = decoder_bias.shape[0]
    part = model // 4
    ff_part = ff_shard * n_dp // 4
    dh_part = dh_shard * n_dp // 4
    room = 2 * slots if n_query > 2 else (2 * slots * 5 // 8 + 15) // 16 * 16 + 16
    dp_index = lax.axis_index("dp").astype(jnp.int32)
    query_index = lax.axis_index("query").astype(jnp.int32)
    core = dp_index % 2
    half = query_index % 2
    quarter = 2 * half + core
    index = jnp.stack([core, half])
    chip = dp_index // 2
    position = jnp.where(chip % 2 == 0, chip // 2, chips - 1 - chip // 2)
    ring = [2 * i for i in range(chips // 2)] + [2 * i + 1 for i in reversed(range(chips // 2))]
    same_line = [[4 * i + k for i in range(n_dp // 4)] for k in range(4)]
    same_core = [[2 * i + k for i in range(chips)] for k in range(2)]
    chip_bits = [1 << i for i in range(1, n_dp.bit_length() - 1)]
    query_bits = [1 << i for i in range(n_query.bit_length() - 1)]

    def ring_moves(step):
        return [
            (2 * ring[i] + k, 2 * ring[(i + step) % chips] + k) for i in range(chips) for k in range(2)
        ]

    ahead, behind = ring_moves(1), ring_moves(-1)

    def dp_swap(value, bit):
        return lax.ppermute(value, "dp", [(i, i ^ bit) for i in range(n_dp)])

    def core_swap(value):
        return dp_swap(value, 1)

    def query_swap(value, bit=1):
        return lax.ppermute(value, "query", [(i, i ^ bit) for i in range(n_query)])

    def gather_four(value):
        near = jnp.stack([value, query_swap(value)], axis=1)
        return jnp.concatenate([near, core_swap(near)], axis=1)

    def scatter_four(value, batches):
        blocks = value.reshape((batches, 4, -1) + value.shape[1:])
        received = core_swap(blocks[:, 2:].astype(BF16))
        far = query_swap((blocks[:, 1] + received[:, 1].astype(F32)).astype(BF16))
        total = blocks[:, 0] + received[:, 0].astype(F32) + far.astype(F32)
        return total.reshape((-1,) + value.shape[1:])

    def order(which, first, second):
        return jnp.where(which == 0, first, second), jnp.where(which == 0, second, first)

    def by_quarter(a, b, c, d):
        a, b = order(core, a, b)
        c, d = order(core, c, d)
        a, c = order(half, a, c)
        b, d = order(half, b, d)
        return [a, b, c, d]

    def exchange_four(blocks):
        own, near, far, both = by_quarter(*blocks)
        theirs = core_swap(jnp.stack([near, both]))
        beyond = query_swap(jnp.stack([far, theirs[1]]))
        return own, theirs[0], beyond[0], beyond[1]

    def ring_start(mine, theirs):
        low, high = order(core, mine, core_swap(theirs))
        return [low, high]

    def last(held):
        return tuple(held[-2:])

    def pin(value, *events):
        return lax.optimization_barrier((value, *events))[0]

    def ring_step(held, *events):
        if len(held) < 2 * chips:
            low, high = lax.optimization_barrier((*last(held), *events))[:2]
            held.append(lax.ppermute(low, "dp", ahead))
            held.append(lax.ppermute(high, "dp", behind))

    def other_pairs(value):
        for bit in query_bits[1:]:
            value = value + query_swap(value, bit)
        return value

    def to_owner(low, high):
        mine, theirs = order(core, low, high)
        theirs = core_swap(theirs)
        far = query_swap(jnp.stack([mine, theirs]))
        return mine, theirs, far[0], far[1]

    def cores(rows):
        return rows[:shard], rows[shard:]

    def chip_rows(mine, theirs):
        return jnp.concatenate(order(core, mine, core_swap(theirs)))

    def plane_gather(rows):
        return lax.all_gather(rows, "dp", axis=0, tiled=True, axis_index_groups=same_core)

    def plane_scatter(grads):
        return lax.psum_scatter(
            grads, "dp", scatter_dimension=0, tiled=True, axis_index_groups=same_core
        )

    def ring_scatter(grads, *lines):
        rows = grads.shape[0] // n_dp

        def piece(offset, side):
            start = (2 * ring_chip(position + offset, chips) + side) * rows
            return lax.dynamic_slice(grads, (start, 0), (rows, grads.shape[1]))

        low, high = piece(-1, 0), piece(1, 1)
        events = ()
        for step in range(1, chips):
            low = lax.ppermute(low, "dp", ahead)
            high = lax.ppermute(high, "dp", behind)
            low = (low.astype(F32) + piece(-1 - step, 0).astype(F32)).astype(BF16)
            high = (high.astype(F32) + piece(1 + step, 1).astype(F32)).astype(BF16)
            low, high = lax.optimization_barrier((low, high, *events))[:2]
            events = ()
            for line in lines:
                events += tuple(line[step - 1](low)) if step <= len(line) else ()
        for line in lines:
            for work in line[chips - 1 :]:
                work(low)
        return other_pairs(low), other_pairs(high)

    def y_half(grads, which):
        held = grads.reshape(-1, 2, 2 * shard, grads.shape[1])
        held = lax.dynamic_index_in_dim(held, which, 1, keepdims=False)
        return held.reshape(-1, grads.shape[1])

    def y_sum(grads, far):
        return (y_half(grads, chip % 2).astype(F32) + far.astype(F32)).astype(BF16)

    def line_scatter(total):
        return lax.psum_scatter(
            total, "dp", scatter_dimension=0, tiled=True, axis_index_groups=same_line
        )

    def group_sum(values):
        values = values + core_swap(values)[:, ::-1]
        return values + query_swap(values)

    first_ring = ring_start(
        *split_attention(
            qkv_weight, out_weight, [attn_gain, ffn_gain, up_bias, decoder_bias, readout], quarter
        )
    )
    ring_step(first_ring)
    pieces = split_rest(
        pin(up_weight, *first_ring[:2]), down_weight, cell_weight, gene_weight, quarter, n_dp
    )
    tokens_far = query_swap(tokens[:, 0])
    cotangent_far = query_swap(pin(out_cotangent, tokens_far)[:, 0])
    gene_own = [gene_embed[batch, 0] for batch in range(micro)]
    gene_far = [query_swap(pin(value, tokens_far)) for value in gene_own]

    def with_cores(own, far):
        near = jnp.stack([own, far], axis=1)
        return jnp.concatenate([near, core_swap(near)], axis=1).reshape(-1, model)

    own_tokens = tokens[:, 0].reshape(micro * length, model)
    for step in range(2, chips):
        arrived = {2: (tokens_far,), chips - 3: (cotangent_far,), chips - 1: (gene_far[0],)}.get(step, ())
        ring_step(first_ring, *arrived)
        if step == chips - 1:
            rows = [pin(chip_rows(*pieces[2 * i : 2 * i + 2]), *last(first_ring)) for i in range(3)]
            up_part, down_part, decoder_part = (plane_gather(value) for value in rows)
        if step == 3:
            all_tokens = [tokens[:, 0], tokens_far]
            all_tokens += [core_swap(value) for value in all_tokens]
    attention_part, vectors = place(first_ring, position, (shard, 8))
    vectors = vectors.reshape(n_dp, 8, model)[:, 0].astype(F32)
    bounds = [0, shard, 2 * shard, 2 * shard + ff_shard, 2 * shard + ff_shard + dh_shard]
    bounds.append(bounds[-1] + dh_shard)
    pieces = [vectors[:, low:high] for low, high in zip(bounds[:-1], bounds[1:])]
    attn_gain_all = pieces[0].reshape(model)
    qkv_part = attention_part[:, : 3 * part]
    out_blocks = attention_part[:, 3 * part :].reshape(4, part, part)
    out_part = jnp.concatenate(
        by_quarter(*exchange_four([out_blocks[i] for i in range(4)])), axis=1
    )

    normed = norm_four(all_tokens, attn_gain_all)
    projected = product(normed, qkv_part).astype(BF16)
    projected = pin(projected, gene_far[-1])
    own_wide = own_tokens.astype(F32)
    mixed, second, hidden, norm_two, scale_two = [], [], [], [], []
    for batch in range(micro):
        mixed.append(attend(projected, length, 4 * batch, 4))
        if batch == 0:
            pieces = [pin(piece, mixed[0]) for piece in pieces]
        partial = product(mixed[-1], out_part)
        projected = pin(projected, partial)
        hidden.append(own_wide[batch * length : (batch + 1) * length] + scatter_four(partial, 1))
    all_cotangent = with_cores(out_cotangent[:, 0], pin(cotangent_far, partial))
    facts = [facts_of(pin(query_live[0, :, 0], partial), query_cell[:, 0], query_label[:, 0])]
    facts.append(query_swap(facts[0]))
    facts += [core_swap(value) for value in facts]
    counts = [jnp.where(half == 0, facts[i][:, 3, 0], facts[i + 1][:, 3, 0]) for i in (0, 2)]
    starts = (jnp.stack(counts, axis=1).reshape(-1).astype(jnp.int32) + 15) // 16 * 16
    facts = line_up(facts, index, starts, room)
    facts = [facts[:, :, i] for i in range(3)]
    gene_near = [pin(value, partial) for value in gene_own + gene_far]
    gene_rows = pack(gene_near + [core_swap(value) for value in gene_near], index, starts, room)
    ffn_gain_all = pieces[1].reshape(model)
    up_bias_part = lax.dynamic_index_in_dim(
        pieces[2].reshape(n_dp, 4, ff_shard // 4), quarter, 1, keepdims=False
    ).reshape(ff_part)
    decoder_bias_part = lax.dynamic_slice(pieces[3].reshape(-1), (quarter * dh_part,), (dh_part,))
    readout_part = lax.dynamic_slice(pieces[4].reshape(-1), (quarter * dh_part,), (dh_part,))
    for batch in range(micro):
        normal, scale = layer_stats(hidden[batch])
        norm_two.append(normal)
        scale_two.append(scale)
        second.append(gather_four((normal * ffn_gain_all).astype(BF16)[None]))
    hidden, norm_two, scale_two = (jnp.concatenate(parts) for parts in (hidden, norm_two, scale_two))
    second = jnp.concatenate(second).reshape(-1, model)
    mixed = jnp.concatenate(mixed)
    up_proj = product(pin(second, gene_rows), up_part) + up_bias_part
    active = jax.nn.gelu(up_proj, approximate=True).astype(BF16)
    branch = product(active, down_part)

    (first_branch_out,) = first_rows_of([branch], length)

    def first_of(rows):
        return rows.reshape((-1, length) + rows.shape[1:])[:, 0]

    first_output = first_of(hidden) + scatter_four(first_branch_out, micro)
    output = (hidden + scatter_four(branch, micro)).reshape(micro, length, model)
    block_out = output.astype(BF16).at[:, 0].set(first_output.astype(BF16))

    gelu_back = jax.vjp(lambda inner: jax.nn.gelu(inner, approximate=True), up_proj)[1]
    grad_down_part = row_product(pin(active, branch), all_cotangent).astype(BF16)
    down_sent = y_half(grad_down_part, 1 - chip % 2)
    down_far = dp_swap(down_sent, 2)
    cotangent_in = pin(all_cotangent, down_sent)
    grad_up_proj = gelu_back(times_transpose(cotangent_in, down_part))[0].astype(BF16)
    grad_up_part = row_product(second, grad_up_proj).astype(BF16)
    up_sent = y_half(grad_up_part, 1 - chip % 2)
    up_far = dp_swap(up_sent, 2)
    grad_second = times_transpose(pin(grad_up_proj, up_sent), up_part)
    grad_second = scatter_four(grad_second, micro)
    down_total = y_sum(grad_down_part, down_far)
    grad_second = pin(grad_second, down_total)
    down_total = line_scatter(down_total)
    cell_part, gene_part = decoder_part[:, :dh_part], decoder_part[:, dh_part:]
    grad_hidden_norm, grad_ffn_gain = norm_back(grad_second, ffn_gain_all, norm_two, scale_two)
    own_cotangent = out_cotangent[:, 0].reshape(micro * length, model).astype(F32)
    grad_hidden = own_cotangent + grad_hidden_norm

    attn_own = grad_hidden.astype(BF16).reshape(micro, length, model)
    attn_far = query_swap(attn_own)

    summaries = first_output.astype(BF16)
    for bit in query_bits:
        summaries = jnp.stack([summaries, query_swap(summaries, bit)])
    summaries = jnp.stack([summaries, core_swap(summaries)])
    cells = 2 * n_query * micro
    summaries = summaries.reshape(cells, model)
    cell_values = product(summaries, cell_part)
    cell_values = cell_values.reshape(2, n_query, micro, dh_part).transpose(2, 0, 1, 3)
    asked = facts[0].astype(jnp.int32) ^ query_index
    chosen_cell = cell_values[:, :, 0, None]
    for i in range(1, n_query):
        chosen_cell = jnp.where(asked[..., None] == i, cell_values[:, :, i, None], chosen_cell)
    asked = (jnp.arange(2)[None, :, None] * n_query + asked) * micro + jnp.arange(micro)[:, None, None]
    onehot = (asked.reshape(-1, 1) == jnp.arange(cells, dtype=jnp.int32)).astype(BF16)
    pre_act = product(pin(gene_rows, attn_own), gene_part).reshape(micro, 2, room, dh_part) + chosen_cell
    pre_act = pre_act + decoder_bias_part
    chance = jax.nn.sigmoid(pre_act)
    activity = pre_act * chance
    logits = jnp.sum(activity * readout_part, axis=-1)
    up_total = y_sum(grad_up_part, pin(up_far, logits))
    attn_near = jnp.stack([attn_own, pin(attn_far, up_total)], axis=1)
    logits = pin(logits, up_total)
    up_total = line_scatter(up_total)
    grad_attn = jnp.concatenate([attn_near, core_swap(attn_near)], axis=1).reshape(-1, model)
    logits = group_sum(logits)
    grad_logits = facts[2] * (jax.nn.sigmoid(logits) - facts[1])
    grad_readout = jnp.sum(grad_logits[..., None] * activity, axis=(0, 1, 2))
    slope = chance * (1.0 + pre_act * (1.0 - chance))
    grad_pre = (grad_logits[..., None] * readout_part * slope).astype(BF16).reshape(-1, dh_part)
    grad_decoder_bias = jnp.sum(grad_pre.astype(F32), axis=0)
    grad_cells = row_product(onehot, grad_pre).astype(BF16)
    grad_summary = times_transpose(grad_cells, cell_part).reshape(2, n_query, micro, model)
    grad_summary = grad_summary[0] + core_swap(grad_summary[1].astype(BF16)).astype(F32)
    grad_gene_part = row_product(gene_rows, pin(grad_pre, grad_summary)).astype(BF16)
    gene_total = plane_scatter(grad_gene_part)
    grad_mixed = times_transpose(grad_attn, out_part).astype(BF16)

    for bit in reversed(query_bits):
        grad_summary = grad_summary.reshape(2, -1, micro, model)
        far = query_swap(grad_summary[1].astype(BF16), bit)
        grad_summary = grad_summary[0] + far.astype(F32)
    grad_summary = grad_summary.reshape(micro, model)

    first_active, first_in, first_proj, first_base, first_cot = first_rows_of(
        [active, second, up_proj, grad_up_proj, all_cotangent], length
    )
    first_cotangent = first_of(own_cotangent)
    first_grad = first_cotangent + grad_summary
    first_branch = gather_four(first_grad.astype(BF16)[:, None]).reshape(-1, model)
    first_change = (first_branch.astype(F32) - first_cot.astype(F32)).astype(BF16)
    first_gelu_back = jax.vjp(
        lambda inner: jax.nn.gelu(inner, approximate=True), first_proj
    )[1]
    first_up = first_gelu_back(times_transpose(first_branch, down_part))[0].astype(BF16)
    first_up_change = (first_up.astype(F32) - first_base.astype(F32)).astype(BF16)
    first_second = scatter_four(times_transpose(first_up, up_part), micro)
    first_norm, first_scale = first_of(norm_two), first_of(scale_two)
    first_hidden, first_gain = norm_back(first_second, ffn_gain_all, first_norm, first_scale)
    first_hidden = first_grad + first_hidden
    first_attn = gather_four(first_hidden.astype(BF16)[:, None]).reshape(-1, model)
    first_mixed = times_transpose(first_attn, out_part).astype(BF16)
    first_attn_base, first_mixed_rows = first_rows_of([grad_attn, mixed], length)
    first_attn_change = (first_attn.astype(F32) - first_attn_base.astype(F32)).astype(BF16)
    grad_up_bias = jnp.sum(grad_up_proj.astype(F32), axis=0) + jnp.sum(
        first_up_change.astype(F32), axis=0
    )
    grad_ffn_gain = grad_ffn_gain + first_gain - jnp.sum(first_of(grad_second) * first_norm, axis=0)
    grad_hidden = grad_hidden.reshape(micro, length, model).at[:, 0].set(first_hidden)
    grad_hidden = grad_hidden.reshape(micro * length, model)

    grad_out_part = row_product(mixed, grad_attn) + row_product(first_mixed_rows, first_attn_change)
    grad_out_part = grad_out_part.astype(BF16)
    out_blocks = exchange_four([grad_out_part[:, i * part : (i + 1) * part] for i in range(4)])
    grad_projected = attend_back(projected, pin(grad_mixed, grad_gene_part), first_mixed[:, None], length)
    grad_qkv_part = row_product(normed, grad_projected).astype(BF16)
    attention_in = paste(grad_qkv_part, out_blocks, index)
    grad_normed = times_transpose(pin(grad_projected, attention_in), qkv_part)
    norm_one, scale_one = layer_stats(own_wide)
    blocks = grad_normed.reshape(micro, 4, length, model)
    received = core_swap(blocks[:, 2:].astype(BF16)).astype(F32)
    near_sum = blocks[:, 0] + received[:, 0]
    far_sum = query_swap((blocks[:, 1] + received[:, 1]).astype(BF16))

    left = jnp.concatenate([first_active, first_in, summaries])[None]
    for bit in chip_bits:
        left = jnp.concatenate([left, dp_swap(left, bit)])
    left = left.reshape(chips, left.shape[1], chips, 2 * shard)
    left = lax.dynamic_index_in_dim(left, chip, 2, keepdims=False)
    travelling = [jnp.concatenate([first_change, first_up_change, grad_cells])[None]]
    owned = {}

    def few_step(bit, event):
        value = pin(travelling[-1], event)
        travelling.append(jnp.concatenate([value, dp_swap(value, bit)]))
        return (travelling[-1],)

    def few_rows(start, stop):
        rows = travelling[-1][:, start:stop].reshape(-1, ff_part)
        return row_product(left[:, start:stop].reshape(-1, 2 * shard), rows)

    def few_sums(event):
        firsts = 4 * micro
        few = jnp.stack([down_total, up_total, jnp.zeros_like(up_total)]).astype(F32)
        few = few + jnp.stack(
            [
                few_rows(0, firsts),
                few_rows(firsts, 2 * firsts),
                few_rows(2 * firsts, 2 * firsts + cells),
            ]
        )
        few = other_pairs(pin(few.astype(BF16), event)).reshape(3, 2, shard, model)
        mine, theirs = order(core, few[:, 0], few[:, 1])
        owned["few"] = mine, core_swap(theirs)
        return owned["few"][1:]

    def few_far(event):
        far = query_swap(pin(jnp.stack(owned["few"]), event))
        owned["few"] = (*owned["few"], far[0], far[1])
        return ()

    def few_here(event):
        return owned["few"][2:]

    sums = {}

    def norm_step(event):
        grad_normed = (near_sum + far_sum.astype(F32)).reshape(micro * length, model)
        grad_input_norm, grad_attn_gain = norm_back(grad_normed, attn_gain_all, norm_one, scale_one)
        sums["tokens"] = (grad_hidden + grad_input_norm).reshape(micro, 1, length, model)
        chosen = (jnp.arange(4) == quarter).astype(F32)
        sums["small"] = jnp.concatenate(
            [
                grad_attn_gain.reshape(n_dp, shard),
                grad_ffn_gain.reshape(n_dp, shard),
                (grad_up_bias.reshape(n_dp, 1, ff_shard // 4) * chosen[:, None]).reshape(n_dp, ff_shard),
                (chosen[:, None] * grad_decoder_bias).reshape(n_dp, dh_shard),
                (chosen[:, None] * grad_readout).reshape(n_dp, dh_shard),
            ],
            axis=1,
        )
        return (sums["small"],)

    def sum_step(bit, event):
        value = pin(sums["small"], event)
        value = value.reshape((2, value.shape[0] // 2) + value.shape[1:])
        kept, sent = order((dp_index // bit) % 2, value[0], value[1])
        sums["small"] = kept + dp_swap(sent, bit)
        return (sums["small"],)

    def sum_query(bit, event):
        value = pin(sums["small"], event)
        sums["small"] = value + query_swap(value, bit)
        return (sums["small"],)

    first_line = [functools.partial(few_step, bit) for bit in chip_bits] + [few_sums, few_far]
    first_line += [few_here] if len(chip_bits) + 3 < chips else []
    second_line = [lambda event: (), lambda event: (far_sum,), norm_step]
    second_line += [functools.partial(sum_step, bit) for bit in reversed([1] + chip_bits)]
    second_line += [functools.partial(sum_query, bit) for bit in query_bits]
    attention_grads = ring_scatter(attention_in, first_line, second_line)
    few_owned = owned["few"]
    gene_owned = to_owner(*cores(other_pairs(gene_total)))
    grad_tokens, vector_sums = sums["tokens"], sums["small"]

    grad_gene = jnp.concatenate(by_quarter(*gene_owned), axis=1).astype(F32)
    down_rows, up_rows, cell_rows = zip(*((block[0], block[1], block[2]) for block in few_owned))
    grad_cell = jnp.concatenate(by_quarter(*cell_rows), axis=1).astype(F32)
    grad_down = jnp.concatenate(by_quarter(*down_rows)).astype(F32)
    (grad_up,) = join(up_rows, index, column_places("up", ff_part, n_dp), [4 * ff_part])
    grad_qkv, grad_out = join(
        to_owner(*attention_grads), index, column_places("attention", part, n_dp), [3 * model, model]
    )

    small = [vector_sums[0, low:high] for low, high in zip(bounds[:-1], bounds[1:])]
    return (
        block_out[:, None],
        grad_tokens,
        grad_qkv,
        grad_out,
        grad_up,
        grad_down,
        small[0],
        small[1],
        small[2],
        grad_cell,
        grad_gene,
        small[3],
        small[4],
    )


def solution(mesh):
    cells = P(None, ("dp", "query"), None, None)
    rows = P("dp", None)
    vector = P("dp")
    slots = P(None, ("dp", "query"), None)
    return jax.shard_map(
        functools.partial(shards, mesh.shape["dp"], mesh.shape["query"]),
        mesh=mesh,
        in_specs=(
            cells, cells, rows, rows, rows, rows, vector, vector, vector, rows, rows, vector, vector,
            cells, slots, slots, P("dp", None, "query"),
        ),
        out_specs=(
            cells, cells, rows, rows, rows, rows, vector, vector, vector, rows, rows, vector, vector,
        ),
        check_vma=False,
    )
```

```python
import functools

import jax
import jax.numpy as jnp
from jax import lax
from jax.experimental import pallas as pl
from jax.experimental.pallas import tpu as pltpu
from jax.sharding import PartitionSpec as P

HEAD = 64
EPSILON = 1e-05
F32 = jnp.float32
BF16 = jnp.bfloat16


def product(left, right):
    return jnp.dot(left, right, preferred_element_type=F32)


def row_product(left, right):
    return lax.dot_general(left, right, (((0,), (0,)), ((), ())), preferred_element_type=F32)


def times_transpose(left, right):
    return lax.dot_general(left, right, (((1,), (1,)), ((), ())), preferred_element_type=F32)


def layer_stats(values):
    average = jnp.mean(values, axis=-1, keepdims=True)
    centred = values - average
    variance = jnp.mean(centred * centred, axis=-1, keepdims=True)
    inverse = lax.rsqrt(variance + EPSILON)
    return (centred * inverse, inverse)


def norm_back(grad_scaled, gain, normal, inverse):
    grad_normal = grad_scaled * gain
    along_normal = jnp.mean(grad_normal * normal, axis=-1, keepdims=True)
    average = jnp.mean(grad_normal, axis=-1, keepdims=True)
    grad_values = inverse * (grad_normal - average - normal * along_normal)
    return (grad_values, jnp.sum(grad_scaled * normal, axis=0))


def norm_kernel(gain_ref, *refs):
    sources, out_ref = refs[:-1], refs[-1]
    micro, length, _ = sources[0].shape
    for batch in range(micro):
        for i, source in enumerate(sources):
            normal, _ = layer_stats(source[batch].astype(F32))
            start = (batch * len(sources) + i) * length
            out_ref[start : start + length, :] = (normal * gain_ref[...]).astype(BF16)


def norm_four(sources, gain):
    micro, length, model = sources[0].shape
    rows = len(sources) * micro * length
    whole = pl.BlockSpec(memory_space=pltpu.VMEM)
    return pl.pallas_call(
        norm_kernel,
        in_specs=[whole] * (1 + len(sources)),
        out_specs=whole,
        out_shape=jax.ShapeDtypeStruct((rows, model), BF16),
        cost_estimate=pl.CostEstimate(
            flops=8 * rows * model, bytes_accessed=4 * rows * model, transcendentals=rows
        ),
        compiler_params=pltpu.CompilerParams(vmem_limit_bytes=32 << 20),
    )(gain[None], *sources)


def softmax_all(scores):
    shifted = [jnp.exp(value - jnp.max(value, axis=-1, keepdims=True)) for value in scores]
    return [value * (1.0 / jnp.sum(value, axis=-1, keepdims=True)) for value in shifted]


def heads_of(ref, width, part):
    return [ref[:, part * width + i : part * width + i + HEAD] for i in range(0, width, HEAD)]


def attend_kernel(projected_ref, mixed_ref):
    width = mixed_ref.shape[1]
    queries, keys, values = (heads_of(projected_ref, width, part) for part in range(3))
    probs = softmax_all([times_transpose(q, k) * 0.125 for q, k in zip(queries, keys)])
    mixed = [product(p.astype(BF16), v).astype(BF16) for p, v in zip(probs, values)]
    for i, value in enumerate(mixed):
        mixed_ref[:, i * HEAD : (i + 1) * HEAD] = value


def attend_back_kernel(projected_ref, grad_mixed_ref, first_ref, grad_ref):
    width = grad_mixed_ref.shape[1]
    is_first = lax.broadcasted_iota(jnp.int32, (grad_mixed_ref.shape[0], width), 0) == 0
    grad_ref[:, 0:width] = jnp.where(is_first, first_ref[0], grad_mixed_ref[...])
    grads = heads_of(grad_ref, width, 0)
    queries, keys, values = (heads_of(projected_ref, width, part) for part in range(3))
    scores = [times_transpose(q, k) * 0.125 for q, k in zip(queries, keys)]
    grad_probs = [times_transpose(g, v) for g, v in zip(grads, values)]
    probs = softmax_all(scores)
    grad_values = [row_product(p.astype(BF16), g) for p, g in zip(probs, grads)]
    along = [jnp.sum(g * p, axis=-1, keepdims=True) for g, p in zip(grad_probs, probs)]
    grad_scores = [
        (p * (g - a) * 0.125).astype(BF16) for p, g, a in zip(probs, grad_probs, along)
    ]
    grad_queries = [product(g, k) for g, k in zip(grad_scores, keys)]
    grad_keys = [row_product(g, q) for g, q in zip(grad_scores, queries)]
    for part, parts in enumerate((grad_queries, grad_keys, grad_values)):
        for i, value in enumerate(parts):
            start = part * width + i * HEAD
            grad_ref[:, start : start + HEAD] = value.astype(BF16)


def attend(projected, length, first, count):
    rows, wide = count * length, projected.shape[1]
    return pl.pallas_call(
        attend_kernel,
        grid=(count,),
        in_specs=[pl.BlockSpec((length, wide), lambda i: (first + i, 0))],
        out_specs=pl.BlockSpec((length, wide // 3), lambda i: (i, 0)),
        out_shape=jax.ShapeDtypeStruct((rows, wide // 3), BF16),
        cost_estimate=pl.CostEstimate(
            flops=4 * rows * length * wide // 3,
            bytes_accessed=rows * wide * 3,
            transcendentals=rows * length * wide // 3 // HEAD,
        ),
    )(projected)


def attend_back(projected, grad_mixed, first, length):
    rows, wide = projected.shape
    return pl.pallas_call(
        attend_back_kernel,
        grid=(rows // length,),
        in_specs=[
            pl.BlockSpec((length, wide), lambda i: (i, 0)),
            pl.BlockSpec((length, wide // 3), lambda i: (i, 0)),
            pl.BlockSpec((1, 1, wide // 3), lambda i: (i, 0, 0)),
        ],
        out_specs=pl.BlockSpec((length, wide), lambda i: (i, 0)),
        out_shape=jax.ShapeDtypeStruct((rows, wide), BF16),
        cost_estimate=pl.CostEstimate(
            flops=10 * rows * length * wide // 3,
            bytes_accessed=rows * wide * 5,
            transcendentals=rows * length * wide // 3 // HEAD,
        ),
    )(projected, grad_mixed, first)


def ring_chip(position, chips):
    position = lax.rem(position + 2 * chips, chips)
    return jnp.where(position < chips // 2, 2 * position, 2 * (chips - 1 - position) + 1)


def place_kernel(segments, position_ref, *refs):
    outs, sems = refs[-1 - len(segments) : -1], refs[-1]
    count = (len(refs) - 1 - len(segments)) // 2
    copies = []
    for step in range(count):
        for side in range(2):
            piece = refs[2 * step + side]
            source = ring_chip(position_ref[0] + (step if side else -step), count)
            begin = 0
            for out, rows in zip(outs, segments):
                start = pl.multiple_of((2 * source + side) * rows, rows)
                copies.append(
                    pltpu.make_async_copy(
                        piece.at[pl.ds(begin, rows), :], out.at[pl.ds(start, rows), :], sems.at[len(copies)]
                    )
                )
                begin += rows
    for copy in copies:
        copy.start()
    for copy in copies:
        copy.wait()


def place(pieces, position, segments):
    tall, wide = pieces[0].shape
    whole = pl.BlockSpec(memory_space=pltpu.VMEM)
    return pl.pallas_call(
        functools.partial(place_kernel, segments),
        in_specs=[pl.BlockSpec(memory_space=pltpu.SMEM)]
        + [pl.BlockSpec(memory_space=pl.ANY)] * len(pieces),
        out_specs=[whole] * len(segments),
        scratch_shapes=[pltpu.SemaphoreType.DMA((len(pieces) * len(segments),))],
        out_shape=[jax.ShapeDtypeStruct((len(pieces) * rows, wide), BF16) for rows in segments],
        cost_estimate=pl.CostEstimate(
            flops=0, bytes_accessed=4 * len(pieces) * tall * wide, transcendentals=0
        ),
        compiler_params=pltpu.CompilerParams(vmem_limit_bytes=32 << 20),
    )(position.reshape(1), *pieces)


def column_places(kind, part, n_dp):
    if kind == "attention":
        model = 4 * part
        return [
            [(0, i * model + k * part, i * part, part) for i in range(3)] + [(1, k * part, 3 * part, part)]
            for k in range(4)
        ]
    width = part // n_dp
    return [[(0, (4 * i + k) * width, i * width, width) for i in range(n_dp)] for k in range(4)]


def join_kernel(places, index_ref, *refs):
    blocks = [ref[...].astype(F32) for ref in refs[:4]]
    core, half = index_ref[0], index_ref[1]

    def swap(index, i, j):
        first = jnp.where(index == 0, blocks[i], blocks[j])
        blocks[j] = jnp.where(index == 0, blocks[j], blocks[i])
        blocks[i] = first

    swap(core, 0, 1)
    swap(core, 2, 3)
    swap(half, 0, 2)
    swap(half, 1, 3)
    for block, moves in zip(blocks, places):
        for output, start, source, width in moves:
            refs[4 + output][:, start : start + width] = block[:, source : source + width]


def join(blocks, index, places, widths):
    rows = blocks[0].shape[0]
    whole = pl.BlockSpec(memory_space=pltpu.VMEM)
    return pl.pallas_call(
        functools.partial(join_kernel, places),
        in_specs=[pl.BlockSpec(memory_space=pltpu.SMEM)] + [whole] * 4,
        out_specs=[whole] * len(widths),
        out_shape=[jax.ShapeDtypeStruct((rows, width), F32) for width in widths],
        cost_estimate=pl.CostEstimate(
            flops=0, bytes_accessed=6 * rows * sum(widths), transcendentals=0
        ),
        compiler_params=pltpu.CompilerParams(vmem_limit_bytes=32 << 20),
    )(index, *blocks)


def split_attention_kernel(index_ref, qkv_ref, out_ref, *refs):
    vectors, targets = refs[:-2], refs[-2:]
    rows, part = out_ref.shape[0], out_ref.shape[1] // 4
    for k in range(4):
        for flip, target in enumerate(targets):

            @pl.when(index_ref[0] == k ^ flip)
            def _():
                for i in range(3):
                    target[0:rows, i * part : (i + 1) * part] = qkv_ref[
                        :, (4 * i + k) * part : (4 * i + k + 1) * part
                    ]
                target[0:rows, 3 * part :] = out_ref[:, k * part : (k + 1) * part]

    for target in targets:
        start = 0
        for vector in vectors:
            width = vector.shape[0]
            target[rows : rows + 1, start : start + width] = vector[...].reshape(1, width)
            start += width


def split_attention(qkv_weight, out_weight, vectors, quarter):
    rows, model = out_weight.shape
    whole = pl.BlockSpec(memory_space=pltpu.VMEM)
    return pl.pallas_call(
        split_attention_kernel,
        in_specs=[pl.BlockSpec(memory_space=pltpu.SMEM)] + [whole] * (2 + len(vectors)),
        out_specs=[whole] * 2,
        out_shape=[jax.ShapeDtypeStruct((rows + 8, model), BF16)] * 2,
        cost_estimate=pl.CostEstimate(
            flops=0, bytes_accessed=12 * rows * model, transcendentals=0
        ),
    )(quarter.reshape(1), qkv_weight, out_weight, *vectors)


def split_rest_kernel(n_dp, index_ref, up_ref, down_ref, cell_ref, gene_ref, *targets):
    wide = cell_ref.shape[1] // 4
    cut = down_ref.shape[0] // 4
    width = wide // n_dp
    for flip in range(2):
        up, down, decoder = targets[flip::2]
        start = pl.multiple_of((index_ref[0] ^ flip) * cut, cut)
        down[...] = down_ref[pl.ds(start, cut), :]
        for k in range(4):

            @pl.when(index_ref[0] == k ^ flip)
            def _():
                for i in range(n_dp):
                    up[:, i * width : (i + 1) * width] = up_ref[
                        :, (4 * i + k) * width : (4 * i + k + 1) * width
                    ]
                decoder[:, :wide] = cell_ref[:, k * wide : (k + 1) * wide]
                decoder[:, wide:] = gene_ref[:, k * wide : (k + 1) * wide]


def split_rest(up_weight, down_weight, cell_weight, gene_weight, quarter, n_dp):
    rows, wide = cell_weight.shape[0], cell_weight.shape[1] // 4
    whole = pl.BlockSpec(memory_space=pltpu.VMEM)
    narrow = jax.ShapeDtypeStruct((rows, wide), BF16)
    shorter = jax.ShapeDtypeStruct((down_weight.shape[0] // 4, down_weight.shape[1]), BF16)
    return pl.pallas_call(
        functools.partial(split_rest_kernel, n_dp),
        in_specs=[pl.BlockSpec(memory_space=pltpu.SMEM)] + [whole] * 4,
        out_specs=[whole] * 6,
        out_shape=[narrow] * 2 + [shorter] * 2 + [jax.ShapeDtypeStruct((rows, 2 * wide), BF16)] * 2,
        cost_estimate=pl.CostEstimate(
            flops=0, bytes_accessed=40 * rows * wide, transcendentals=0
        ),
        compiler_params=pltpu.CompilerParams(vmem_limit_bytes=32 << 20),
    )(quarter.reshape(1), up_weight, down_weight, cell_weight, gene_weight)


def first_kernel(*refs):
    count = len(refs) // 2
    for source, target in zip(refs[:count], refs[count:]):
        for i in range(source.shape[0]):
            target[i : i + 1, :] = source[i, 0:1, :]


def first_rows_of(values, length):
    cells = values[0].shape[0] // length
    values = [value.reshape(cells, length, value.shape[1]) for value in values]
    specs = [pl.BlockSpec((cells, 16, value.shape[2]), lambda i: (0, 0, 0)) for value in values]
    outs = [pl.BlockSpec((cells, value.shape[2]), lambda i: (0, 0)) for value in values]
    return pl.pallas_call(
        first_kernel,
        grid=(1,),
        in_specs=specs,
        out_specs=outs,
        out_shape=[jax.ShapeDtypeStruct((cells, value.shape[2]), value.dtype) for value in values],
        cost_estimate=pl.CostEstimate(
            flops=0, bytes_accessed=64 * cells * sum(value.shape[2] for value in values), transcendentals=0
        ),
    )(*values)


def pack_kernel(room, index_ref, starts_ref, *refs):
    sources, out_ref = refs[:-1], refs[-1]
    micro = len(sources) // 4
    slots = sources[0].shape[0]
    for pair in range(2):
        for batch in range(micro):
            segment = (batch * 2 + pair) * room
            start = starts_ref[batch * 2 + pair]

            def put(first, second):
                kept = min(room, slots)
                out_ref[segment : segment + kept, :] = first[0:kept, :]

                def move(i, carry):
                    source = pl.multiple_of(jnp.minimum(i * 16, slots - 16), 16)
                    target = pl.multiple_of(segment + start + i * 16, 16)
                    out_ref[pl.ds(target, 16), :] = second[pl.ds(source, 16), :]
                    return carry

                lax.fori_loop(0, (room - start) // 16, move, 0)

            own = sources[2 * pair * micro + batch]
            far = sources[(2 * pair + 1) * micro + batch]
            pl.when(index_ref[1] == 0)(functools.partial(put, own, far))
            pl.when(index_ref[1] == 1)(functools.partial(put, far, own))


def pack(sources, index, starts, room):
    model = sources[0].shape[1]
    whole = pl.BlockSpec(memory_space=pltpu.VMEM)
    scalars = pl.BlockSpec(memory_space=pltpu.SMEM)
    total = len(sources) // 2 * room
    return pl.pallas_call(
        functools.partial(pack_kernel, room),
        in_specs=[scalars, scalars] + [whole] * len(sources),
        out_specs=whole,
        out_shape=jax.ShapeDtypeStruct((total, model), BF16),
        cost_estimate=pl.CostEstimate(flops=0, bytes_accessed=5 * total * model, transcendentals=0),
        compiler_params=pltpu.CompilerParams(vmem_limit_bytes=40 << 20),
    )(index, starts, *sources)


def facts_kernel(live_ref, cell_ref, label_ref, out_ref):
    micro, slots = cell_ref.shape
    lane = lax.broadcasted_iota(jnp.int32, (1, slots), 1)
    for batch in range(micro):
        out_ref[batch, 0:1, :] = cell_ref[batch : batch + 1, :].astype(F32)
        out_ref[batch, 1:2, :] = label_ref[batch : batch + 1, :].astype(F32)
        out_ref[batch, 2:3, :] = (lane < live_ref[batch]).astype(F32)
        out_ref[batch, 3:8, :] = jnp.full((5, slots), live_ref[batch], jnp.int32).astype(F32)


def facts_of(live, cell, label):
    whole = pl.BlockSpec(memory_space=pltpu.VMEM)
    return pl.pallas_call(
        facts_kernel,
        in_specs=[pl.BlockSpec(memory_space=pltpu.SMEM)] + [whole] * 2,
        out_specs=whole,
        out_shape=jax.ShapeDtypeStruct((cell.shape[0], 8, cell.shape[1]), F32),
        cost_estimate=pl.CostEstimate(flops=0, bytes_accessed=40 * cell.size, transcendentals=0),
    )(live, cell, label)


def line_kernel(index_ref, starts_ref, *refs):
    sources, out_ref = refs[:4], refs[4]
    micro, facts, slots = sources[0].shape
    room = out_ref.shape[3]
    wide = -(-(room + slots) // 128) * 128
    lane = lax.broadcasted_iota(jnp.int32, (facts, wide), 1)
    beyond = jnp.zeros((facts, wide - slots), F32)
    for batch in range(micro):
        for pair in range(2):
            own, far = sources[2 * pair][batch], sources[2 * pair + 1][batch]
            first = jnp.where(index_ref[1] == 0, own, far)
            second = jnp.where(index_ref[1] == 0, far, own)
            start = starts_ref[2 * batch + pair]
            moved = pltpu.roll(jnp.concatenate([second, beyond], axis=1), start, 1)
            line = jnp.where(lane < start, jnp.concatenate([first, beyond], axis=1), moved)
            out_ref[batch, pair] = line[:, :room]


def line_up(sources, index, starts, room):
    micro, facts, slots = sources[0].shape
    whole = pl.BlockSpec(memory_space=pltpu.VMEM)
    scalars = pl.BlockSpec(memory_space=pltpu.SMEM)
    return pl.pallas_call(
        functools.partial(line_kernel),
        in_specs=[scalars, scalars] + [whole] * 4,
        out_specs=whole,
        out_shape=jax.ShapeDtypeStruct((micro, 2, facts, room), F32),
        cost_estimate=pl.CostEstimate(
            flops=0, bytes_accessed=64 * micro * facts * slots, transcendentals=0
        ),
    )(index, starts, *sources)


def paste_kernel(index_ref, qkv_ref, *refs):
    blocks = [ref[...] for ref in refs[:4]]
    out_ref = refs[4]
    core, half = index_ref[0], index_ref[1]
    wide, part = qkv_ref.shape[1], blocks[0].shape[0]

    def swap(index, i, j):
        first = jnp.where(index == 0, blocks[i], blocks[j])
        blocks[j] = jnp.where(index == 0, blocks[j], blocks[i])
        blocks[i] = first

    swap(core, 0, 1)
    swap(core, 2, 3)
    swap(half, 0, 2)
    swap(half, 1, 3)
    out_ref[:, 0:wide] = qkv_ref[...]
    for i, block in enumerate(blocks):
        out_ref[i * part : (i + 1) * part, wide:] = block


def paste(grad_qkv, blocks, index):
    rows, wide = grad_qkv.shape
    whole = pl.BlockSpec(memory_space=pltpu.VMEM)
    return pl.pallas_call(
        paste_kernel,
        in_specs=[pl.BlockSpec(memory_space=pltpu.SMEM)] + [whole] * 5,
        out_specs=whole,
        out_shape=jax.ShapeDtypeStruct((rows, wide + blocks[0].shape[1]), BF16),
        cost_estimate=pl.CostEstimate(
            flops=0, bytes_accessed=6 * rows * wide, transcendentals=0
        ),
        compiler_params=pltpu.CompilerParams(vmem_limit_bytes=32 << 20),
    )(index, grad_qkv, *blocks)


def shards(
    n_dp,
    n_query,
    tokens,
    out_cotangent,
    qkv_weight,
    out_weight,
    up_weight,
    down_weight,
    attn_gain,
    ffn_gain,
    up_bias,
    cell_weight,
    gene_weight,
    decoder_bias,
    readout,
    gene_embed,
    query_cell,
    query_label,
    query_live,
):
    micro, _, length, model = tokens.shape
    slots = gene_embed.shape[2]
    chips = n_dp // 2
    shard = model // n_dp
    ff_shard = up_bias.shape[0]
    dh_shard = decoder_bias.shape[0]
    part = model // 4
    ff_part = ff_shard * n_dp // 4
    dh_part = dh_shard * n_dp // 4
    room = 2 * slots if n_query > 2 else (2 * slots * 5 // 8 + 15) // 16 * 16 + 16
    dp_index = lax.axis_index("dp").astype(jnp.int32)
    query_index = lax.axis_index("query").astype(jnp.int32)
    core = dp_index % 2
    half = query_index % 2
    quarter = 2 * half + core
    index = jnp.stack([core, half])
    chip = dp_index // 2
    position = jnp.where(chip % 2 == 0, chip // 2, chips - 1 - chip // 2)
    ring = [2 * i for i in range(chips // 2)] + [2 * i + 1 for i in reversed(range(chips // 2))]
    same_line = [[4 * i + k for i in range(n_dp // 4)] for k in range(4)]
    same_core = [[2 * i + k for i in range(chips)] for k in range(2)]
    chip_bits = [1 << i for i in range(1, n_dp.bit_length() - 1)]
    query_bits = [1 << i for i in range(n_query.bit_length() - 1)]

    def ring_moves(step):
        return [
            (2 * ring[i] + k, 2 * ring[(i + step) % chips] + k) for i in range(chips) for k in range(2)
        ]

    ahead, behind = ring_moves(1), ring_moves(-1)

    def dp_swap(value, bit):
        return lax.ppermute(value, "dp", [(i, i ^ bit) for i in range(n_dp)])

    def core_swap(value):
        return dp_swap(value, 1)

    def query_swap(value, bit=1):
        return lax.ppermute(value, "query", [(i, i ^ bit) for i in range(n_query)])

    def gather_four(value):
        near = jnp.stack([value, query_swap(value)], axis=1)
        return jnp.concatenate([near, core_swap(near)], axis=1)

    def scatter_four(value, batches):
        blocks = value.reshape((batches, 4, -1) + value.shape[1:])
        received = core_swap(blocks[:, 2:].astype(BF16))
        far = query_swap((blocks[:, 1] + received[:, 1].astype(F32)).astype(BF16))
        total = blocks[:, 0] + received[:, 0].astype(F32) + far.astype(F32)
        return total.reshape((-1,) + value.shape[1:])

    def order(which, first, second):
        return jnp.where(which == 0, first, second), jnp.where(which == 0, second, first)

    def by_quarter(a, b, c, d):
        a, b = order(core, a, b)
        c, d = order(core, c, d)
        a, c = order(half, a, c)
        b, d = order(half, b, d)
        return [a, b, c, d]

    def exchange_four(blocks):
        own, near, far, both = by_quarter(*blocks)
        theirs = core_swap(jnp.stack([near, both]))
        beyond = query_swap(jnp.stack([far, theirs[1]]))
        return own, theirs[0], beyond[0], beyond[1]

    def ring_start(mine, theirs):
        low, high = order(core, mine, core_swap(theirs))
        return [low, high]

    def last(held):
        return tuple(held[-2:])

    def pin(value, *events):
        return lax.optimization_barrier((value, *events))[0]

    def ring_step(held, *events):
        if len(held) < 2 * chips:
            low, high = lax.optimization_barrier((*last(held), *events))[:2]
            held.append(lax.ppermute(low, "dp", ahead))
            held.append(lax.ppermute(high, "dp", behind))

    def other_pairs(value):
        for bit in query_bits[1:]:
            value = value + query_swap(value, bit)
        return value

    def to_owner(low, high):
        mine, theirs = order(core, low, high)
        theirs = core_swap(theirs)
        far = query_swap(jnp.stack([mine, theirs]))
        return mine, theirs, far[0], far[1]

    def cores(rows):
        return rows[:shard], rows[shard:]

    def chip_rows(mine, theirs):
        return jnp.concatenate(order(core, mine, core_swap(theirs)))

    def plane_gather(rows):
        return lax.all_gather(rows, "dp", axis=0, tiled=True, axis_index_groups=same_core)

    def plane_scatter(grads):
        return lax.psum_scatter(
            grads, "dp", scatter_dimension=0, tiled=True, axis_index_groups=same_core
        )

    def y_half(grads, which):
        held = grads.reshape(-1, 2, 2 * shard, grads.shape[1])
        held = lax.dynamic_index_in_dim(held, which, 1, keepdims=False)
        return held.reshape(-1, grads.shape[1])

    def y_sum(grads, far):
        return (y_half(grads, chip % 2).astype(F32) + far.astype(F32)).astype(BF16)

    def line_scatter(total):
        return lax.psum_scatter(
            total, "dp", scatter_dimension=0, tiled=True, axis_index_groups=same_line
        )

    def group_sum(values):
        values = values + core_swap(values)[:, ::-1]
        return values + query_swap(values)

    first_ring = ring_start(
        *split_attention(
            qkv_weight, out_weight, [attn_gain, ffn_gain, up_bias, decoder_bias, readout], quarter
        )
    )
    ring_step(first_ring)
    pieces = split_rest(
        pin(up_weight, *first_ring[:2]), down_weight, cell_weight, gene_weight, quarter, n_dp
    )
    tokens_far = query_swap(tokens[:, 0])
    cotangent_far = query_swap(pin(out_cotangent, tokens_far)[:, 0])
    gene_own = [gene_embed[batch, 0] for batch in range(micro)]
    gene_far = [query_swap(pin(value, tokens_far)) for value in gene_own]

    def with_cores(own, far):
        near = jnp.stack([own, far], axis=1)
        return jnp.concatenate([near, core_swap(near)], axis=1).reshape(-1, model)

    own_tokens = tokens[:, 0].reshape(micro * length, model)
    for step in range(2, chips):
        arrived = {2: (tokens_far,), chips - 3: (cotangent_far,), chips - 1: (gene_far[0],)}.get(step, ())
        ring_step(first_ring, *arrived)
        if step == chips - 1:
            rows = [pin(chip_rows(*pieces[2 * i : 2 * i + 2]), *last(first_ring)) for i in range(3)]
            up_part, down_part, decoder_part = (plane_gather(value) for value in rows)
        if step == 3:
            all_tokens = [tokens[:, 0], tokens_far]
            all_tokens += [core_swap(value) for value in all_tokens]
    attention_part, vectors = place(first_ring, position, (shard, 8))
    vectors = vectors.reshape(n_dp, 8, model)[:, 0].astype(F32)
    bounds = [0, shard, 2 * shard, 2 * shard + ff_shard, 2 * shard + ff_shard + dh_shard]
    bounds.append(bounds[-1] + dh_shard)
    pieces = [vectors[:, low:high] for low, high in zip(bounds[:-1], bounds[1:])]
    attn_gain_all = pieces[0].reshape(model)
    qkv_part = attention_part[:, : 3 * part]
    out_blocks = attention_part[:, 3 * part :].reshape(4, part, part)
    out_part = jnp.concatenate(
        by_quarter(*exchange_four([out_blocks[i] for i in range(4)])), axis=1
    )

    normed = norm_four(all_tokens, attn_gain_all)
    projected = product(normed, qkv_part).astype(BF16)
    projected = pin(projected, gene_far[-1])
    own_wide = own_tokens.astype(F32)
    mixed, second, hidden, norm_two, scale_two = [], [], [], [], []
    for batch in range(micro):
        mixed.append(attend(projected, length, 4 * batch, 4))
        if batch == 0:
            pieces = [pin(piece, mixed[0]) for piece in pieces]
        partial = product(mixed[-1], out_part)
        projected = pin(projected, partial)
        hidden.append(own_wide[batch * length : (batch + 1) * length] + scatter_four(partial, 1))
    all_cotangent = with_cores(out_cotangent[:, 0], pin(cotangent_far, partial))
    facts = [facts_of(pin(query_live[0, :, 0], partial), query_cell[:, 0], query_label[:, 0])]
    facts.append(query_swap(facts[0]))
    facts += [core_swap(value) for value in facts]
    counts = [jnp.where(half == 0, facts[i][:, 3, 0], facts[i + 1][:, 3, 0]) for i in (0, 2)]
    starts = (jnp.stack(counts, axis=1).reshape(-1).astype(jnp.int32) + 15) // 16 * 16
    facts = line_up(facts, index, starts, room)
    facts = [facts[:, :, i] for i in range(3)]
    gene_near = [pin(value, partial) for value in gene_own + gene_far]
    gene_rows = pack(gene_near + [core_swap(value) for value in gene_near], index, starts, room)
    ffn_gain_all = pieces[1].reshape(model)
    up_bias_part = lax.dynamic_index_in_dim(
        pieces[2].reshape(n_dp, 4, ff_shard // 4), quarter, 1, keepdims=False
    ).reshape(ff_part)
    decoder_bias_part = lax.dynamic_slice(pieces[3].reshape(-1), (quarter * dh_part,), (dh_part,))
    readout_part = lax.dynamic_slice(pieces[4].reshape(-1), (quarter * dh_part,), (dh_part,))
    for batch in range(micro):
        normal, scale = layer_stats(hidden[batch])
        norm_two.append(normal)
        scale_two.append(scale)
        second.append(gather_four((normal * ffn_gain_all).astype(BF16)[None]))
    hidden, norm_two, scale_two = (jnp.concatenate(parts) for parts in (hidden, norm_two, scale_two))
    second = jnp.concatenate(second).reshape(-1, model)
    mixed = jnp.concatenate(mixed)
    up_proj = product(pin(second, gene_rows), up_part) + up_bias_part
    active = jax.nn.gelu(up_proj, approximate=True).astype(BF16)
    branch = product(active, down_part)

    (first_branch_out,) = first_rows_of([branch], length)

    def first_of(rows):
        return rows.reshape((-1, length) + rows.shape[1:])[:, 0]

    first_output = first_of(hidden) + scatter_four(first_branch_out, micro)
    output = (hidden + scatter_four(branch, micro)).reshape(micro, length, model)
    block_out = output.astype(BF16).at[:, 0].set(first_output.astype(BF16))

    gelu_back = jax.vjp(lambda inner: jax.nn.gelu(inner, approximate=True), up_proj)[1]
    grad_down_part = row_product(pin(active, branch), all_cotangent).astype(BF16)
    down_sent = y_half(grad_down_part, 1 - chip % 2)
    down_far = dp_swap(down_sent, 2)
    cotangent_in = pin(all_cotangent, down_sent)
    grad_up_proj = gelu_back(times_transpose(cotangent_in, down_part))[0].astype(BF16)
    grad_up_part = row_product(second, grad_up_proj).astype(BF16)
    up_sent = y_half(grad_up_part, 1 - chip % 2)
    up_far = dp_swap(up_sent, 2)
    grad_second = times_transpose(pin(grad_up_proj, up_sent), up_part)
    grad_second = scatter_four(grad_second, micro)
    down_total = y_sum(grad_down_part, down_far)
    grad_second = pin(grad_second, down_total)
    down_total = line_scatter(down_total)
    cell_part, gene_part = decoder_part[:, :dh_part], decoder_part[:, dh_part:]
    grad_hidden_norm, grad_ffn_gain = norm_back(grad_second, ffn_gain_all, norm_two, scale_two)
    own_cotangent = out_cotangent[:, 0].reshape(micro * length, model).astype(F32)
    grad_hidden = own_cotangent + grad_hidden_norm

    attn_own = grad_hidden.astype(BF16).reshape(micro, length, model)
    attn_far = query_swap(attn_own)

    summaries = first_output.astype(BF16)
    for bit in query_bits:
        summaries = jnp.stack([summaries, query_swap(summaries, bit)])
    summaries = jnp.stack([summaries, core_swap(summaries)])
    cells = 2 * n_query * micro
    summaries = summaries.reshape(cells, model)
    cell_values = product(summaries, cell_part)
    cell_values = cell_values.reshape(2, n_query, micro, dh_part).transpose(2, 0, 1, 3)
    asked = facts[0].astype(jnp.int32) ^ query_index
    chosen_cell = cell_values[:, :, 0, None]
    for i in range(1, n_query):
        chosen_cell = jnp.where(asked[..., None] == i, cell_values[:, :, i, None], chosen_cell)
    asked = (jnp.arange(2)[None, :, None] * n_query + asked) * micro + jnp.arange(micro)[:, None, None]
    onehot = (asked.reshape(-1, 1) == jnp.arange(cells, dtype=jnp.int32)).astype(BF16)
    pre_act = product(pin(gene_rows, attn_own), gene_part).reshape(micro, 2, room, dh_part) + chosen_cell
    pre_act = pre_act + decoder_bias_part
    chance = jax.nn.sigmoid(pre_act)
    activity = pre_act * chance
    logits = jnp.sum(activity * readout_part, axis=-1)
    up_total = y_sum(grad_up_part, pin(up_far, logits))
    attn_near = jnp.stack([attn_own, pin(attn_far, up_total)], axis=1)
    logits = pin(logits, up_total)
    up_total = line_scatter(up_total)
    grad_attn = jnp.concatenate([attn_near, core_swap(attn_near)], axis=1).reshape(-1, model)
    logits = group_sum(logits)
    grad_logits = facts[2] * (jax.nn.sigmoid(logits) - facts[1])
    grad_readout = jnp.sum(grad_logits[..., None] * activity, axis=(0, 1, 2))
    slope = chance * (1.0 + pre_act * (1.0 - chance))
    grad_pre = (grad_logits[..., None] * readout_part * slope).astype(BF16).reshape(-1, dh_part)
    grad_decoder_bias = jnp.sum(grad_pre.astype(F32), axis=0)
    grad_cells = row_product(onehot, grad_pre).astype(BF16)
    grad_summary = times_transpose(grad_cells, cell_part).reshape(2, n_query, micro, model)
    grad_summary = grad_summary[0] + core_swap(grad_summary[1].astype(BF16)).astype(F32)
    grad_gene_part = row_product(gene_rows, pin(grad_pre, grad_summary)).astype(BF16)
    gene_total = plane_scatter(grad_gene_part)
    grad_mixed = times_transpose(grad_attn, out_part).astype(BF16)

    for bit in reversed(query_bits):
        grad_summary = grad_summary.reshape(2, -1, micro, model)
        far = query_swap(grad_summary[1].astype(BF16), bit)
        grad_summary = grad_summary[0] + far.astype(F32)
    grad_summary = grad_summary.reshape(micro, model)

    first_active, first_in, first_proj, first_base, first_cot = first_rows_of(
        [active, second, up_proj, grad_up_proj, all_cotangent], length
    )
    first_cotangent = first_of(own_cotangent)
    first_grad = first_cotangent + grad_summary
    first_branch = gather_four(first_grad.astype(BF16)[:, None]).reshape(-1, model)
    first_change = (first_branch.astype(F32) - first_cot.astype(F32)).astype(BF16)
    first_gelu_back = jax.vjp(
        lambda inner: jax.nn.gelu(inner, approximate=True), first_proj
    )[1]
    first_up = first_gelu_back(times_transpose(first_branch, down_part))[0].astype(BF16)
    first_up_change = (first_up.astype(F32) - first_base.astype(F32)).astype(BF16)
    first_second = scatter_four(times_transpose(first_up, up_part), micro)
    first_norm, first_scale = first_of(norm_two), first_of(scale_two)
    first_hidden, first_gain = norm_back(first_second, ffn_gain_all, first_norm, first_scale)
    first_hidden = first_grad + first_hidden
    first_attn = gather_four(first_hidden.astype(BF16)[:, None]).reshape(-1, model)
    first_mixed = times_transpose(first_attn, out_part).astype(BF16)
    first_attn_base, first_mixed_rows = first_rows_of([grad_attn, mixed], length)
    first_attn_change = (first_attn.astype(F32) - first_attn_base.astype(F32)).astype(BF16)
    grad_up_bias = jnp.sum(grad_up_proj.astype(F32), axis=0) + jnp.sum(
        first_up_change.astype(F32), axis=0
    )
    grad_ffn_gain = grad_ffn_gain + first_gain - jnp.sum(first_of(grad_second) * first_norm, axis=0)
    grad_hidden = grad_hidden.reshape(micro, length, model).at[:, 0].set(first_hidden)
    grad_hidden = grad_hidden.reshape(micro * length, model)

    grad_out_part = row_product(mixed, grad_attn) + row_product(first_mixed_rows, first_attn_change)
    grad_out_part = grad_out_part.astype(BF16)
    out_blocks = exchange_four([grad_out_part[:, i * part : (i + 1) * part] for i in range(4)])
    grad_projected = attend_back(projected, pin(grad_mixed, grad_gene_part), first_mixed[:, None], length)
    grad_qkv_part = row_product(normed, grad_projected).astype(BF16)
    attention_in = paste(grad_qkv_part, out_blocks, index)
    attention_sent = y_half(attention_in, 1 - chip % 2)
    attention_far = dp_swap(attention_sent, 2)
    grad_normed = times_transpose(pin(grad_projected, attention_sent), qkv_part)
    norm_one, scale_one = layer_stats(own_wide)
    blocks = grad_normed.reshape(micro, 4, length, model)
    received = core_swap(blocks[:, 2:].astype(BF16)).astype(F32)
    near_sum = blocks[:, 0] + received[:, 0]
    far_sum = query_swap((blocks[:, 1] + received[:, 1]).astype(BF16))

    left = jnp.concatenate([first_active, first_in, summaries])[None]
    for bit in chip_bits:
        left = jnp.concatenate([left, dp_swap(left, bit)])
    left = left.reshape(chips, left.shape[1], chips, 2 * shard)
    left = lax.dynamic_index_in_dim(left, chip, 2, keepdims=False)
    travelling = [jnp.concatenate([first_change, first_up_change, grad_cells])[None]]
    owned = {}

    def few_step(bit, event):
        value = pin(travelling[-1], event)
        travelling.append(jnp.concatenate([value, dp_swap(value, bit)]))
        return (travelling[-1],)

    def few_rows(start, stop):
        rows = travelling[-1][:, start:stop].reshape(-1, ff_part)
        return row_product(left[:, start:stop].reshape(-1, 2 * shard), rows)

    def few_sums(event):
        firsts = 4 * micro
        few = jnp.stack([down_total, up_total, jnp.zeros_like(up_total)]).astype(F32)
        few = few + jnp.stack(
            [
                few_rows(0, firsts),
                few_rows(firsts, 2 * firsts),
                few_rows(2 * firsts, 2 * firsts + cells),
            ]
        )
        few = other_pairs(pin(few.astype(BF16), event)).reshape(3, 2, shard, model)
        mine, theirs = order(core, few[:, 0], few[:, 1])
        owned["few"] = mine, core_swap(theirs)
        return owned["few"][1:]

    def few_far(event):
        far = query_swap(pin(jnp.stack(owned["few"]), event))
        owned["few"] = (*owned["few"], far[0], far[1])
        return ()

    def few_here(event):
        return owned["few"][2:]

    sums = {}

    def norm_step(event):
        grad_normed = (near_sum + far_sum.astype(F32)).reshape(micro * length, model)
        grad_input_norm, grad_attn_gain = norm_back(grad_normed, attn_gain_all, norm_one, scale_one)
        sums["tokens"] = (grad_hidden + grad_input_norm).reshape(micro, 1, length, model)
        chosen = (jnp.arange(4) == quarter).astype(F32)
        sums["small"] = jnp.concatenate(
            [
                grad_attn_gain.reshape(n_dp, shard),
                grad_ffn_gain.reshape(n_dp, shard),
                (grad_up_bias.reshape(n_dp, 1, ff_shard // 4) * chosen[:, None]).reshape(n_dp, ff_shard),
                (chosen[:, None] * grad_decoder_bias).reshape(n_dp, dh_shard),
                (chosen[:, None] * grad_readout).reshape(n_dp, dh_shard),
            ],
            axis=1,
        )
        return (sums["small"],)

    def sum_step(bit, event):
        value = pin(sums["small"], event)
        value = value.reshape((2, value.shape[0] // 2) + value.shape[1:])
        kept, sent = order((dp_index // bit) % 2, value[0], value[1])
        sums["small"] = kept + dp_swap(sent, bit)
        return (sums["small"],)

    def sum_query(bit, event):
        value = pin(sums["small"], event)
        sums["small"] = value + query_swap(value, bit)
        return (sums["small"],)

    few_step(chip_bits[0], attention_sent)
    few_step(chip_bits[1], travelling[-1])
    attention_total = y_sum(attention_in, pin(attention_far, travelling[-1]))
    for bit in chip_bits[2:]:
        few_step(bit, attention_total)
    attention_rows = line_scatter(attention_total)
    few_sums(travelling[-1])
    few_far(owned["few"][1])
    norm_step(far_sum)
    for bit in reversed([1] + chip_bits):
        sum_step(bit, sums["small"])
    for bit in query_bits:
        sum_query(bit, sums["small"])
    attention_rows = pin(attention_rows, *owned["few"][2:], sums["small"])
    attention_grads = cores(other_pairs(attention_rows))
    few_owned = owned["few"]
    gene_owned = to_owner(*cores(other_pairs(gene_total)))
    grad_tokens, vector_sums = sums["tokens"], sums["small"]

    grad_gene = jnp.concatenate(by_quarter(*gene_owned), axis=1).astype(F32)
    down_rows, up_rows, cell_rows = zip(*((block[0], block[1], block[2]) for block in few_owned))
    grad_cell = jnp.concatenate(by_quarter(*cell_rows), axis=1).astype(F32)
    grad_down = jnp.concatenate(by_quarter(*down_rows)).astype(F32)
    (grad_up,) = join(up_rows, index, column_places("up", ff_part, n_dp), [4 * ff_part])
    grad_qkv, grad_out = join(
        to_owner(*attention_grads), index, column_places("attention", part, n_dp), [3 * model, model]
    )

    small = [vector_sums[0, low:high] for low, high in zip(bounds[:-1], bounds[1:])]
    return (
        block_out[:, None],
        grad_tokens,
        grad_qkv,
        grad_out,
        grad_up,
        grad_down,
        small[0],
        small[1],
        small[2],
        grad_cell,
        grad_gene,
        small[3],
        small[4],
    )


def solution(mesh):
    cells = P(None, ("dp", "query"), None, None)
    rows = P("dp", None)
    vector = P("dp")
    slots = P(None, ("dp", "query"), None)
    return jax.shard_map(
        functools.partial(shards, mesh.shape["dp"], mesh.shape["query"]),
        mesh=mesh,
        in_specs=(
            cells, cells, rows, rows, rows, rows, vector, vector, vector, rows, rows, vector, vector,
            cells, slots, slots, P("dp", None, "query"),
        ),
        out_specs=(
            cells, cells, rows, rows, rows, rows, vector, vector, vector, rows, rows, vector, vector,
        ),
        check_vma=False,
    )
```
